512 devices in a mesh: slab: 64 (over x, y, z_lo), grp: 8 (over z_hi, core).
Axes of the slice: x: 4, y: 8, z: 8 (z_hi: 4, z_lo: 2; z = z_hi * 2 + z_lo), core: 2. Of those that a mesh axis runs over, the one named last changes fastest.
Arguments:
- echo_data: bfloat16 [64, 1024, 2048], P('slab', 'grp'), may hold values from -6 to 6
- acquirer: int32 [3], replicated, may hold values from 0 to 63, as said below
- panels: bfloat16 [64, 3, 64, 128, 128], P('slab', None, 'grp'), may hold values from -0.00390625 to 0.00390625
- block_count: int32 [64, 3], P('slab'), may hold values from 16 to 64, as said below
- block_rows: int32 [64, 3, 64], P('slab'), may hold values from 0 to 7
- block_columns: int32 [64, 3, 64], P('slab'), may hold values from 0 to 15
- apodization: float32 [16, 1024], P(None, 'grp'), may hold values from 0.25 to 2.5
- window_index: int32 [65536], P('slab'), may hold values from 0 to 15
Outputs:
- image: float32 [65536], P(('slab', 'grp'))
The draws below stay inside these ranges and needn't reach their ends.
Inputs may be any that keep to these rules, and one draw needn't show every extreme that they name: `acquirer`: 3 distinct slab indices, the last slab index always among them. `block_count`: slots below the count are live, the others unused; some slab and transmit has all 64 live in every draw.
All inputs are finite; a program needn't handle non-finite values.
Results may differ from the reference program's by a relative error of at most 0.0003.
Values may be sent and summed in bfloat16 or wider, within the bound.
No kernel may reach another device: no remote copies, remote signals or barrier semaphores. Data moves between devices by JAX's collectives and lax.ppermute only.
A program may use at most 128 MiB of HBM per device.

```python
import math
import jax
import jax.numpy as jnp
from jax import lax

CHAN = 1024
SAMPLES = 2048
BLK = 128
TX = 3
NWIN = 16
RB = 8
SB = 16
NB = 64
VOX_SLAB = 1024
VOXELS = 65536
N_SLAB = 64


def draw_acquirer(key, part):
    others = jax.random.permutation(jax.random.fold_in(key, 3), N_SLAB - 1)[:TX - 1]
    values = jnp.concatenate([others.astype(jnp.int32), jnp.full((1,), N_SLAB - 1, jnp.int32)])
    order = jax.random.permutation(jax.random.fold_in(key, 4), TX)
    return values[order].astype(jnp.int32)


def draw_block_count(key, part):
    counts_drawn = jax.random.randint(jax.random.fold_in(key, 1), (N_SLAB, TX), NB // 4, NB + 1)
    busiest = jax.random.randint(jax.random.fold_in(key, 2), (), 0, N_SLAB)
    return counts_drawn.at[busiest, 0].set(NB).astype(jnp.int32)


def with_ends(result, own_key, low, top_value):
    extent = result.shape
    spot = [jax.random.randint(jax.random.fold_in(own_key, axis), (), 0, extent[axis]) for axis in range(len(extent))]
    result = result.at[tuple(spot)].set(low)
    longest = extent.index(max(extent))
    spot[longest] = (spot[longest] + 1) % extent[longest]
    return result.at[tuple(spot)].set(top_value)


def shard_levels(stream_key, shape, cuts, least, top_value):
    gain, own = 1.0, jax.random.fold_in(stream_key, 6)
    for dim, blocks in cuts:
        steps = jnp.exp(jax.random.uniform(jax.random.fold_in(own, dim), (blocks,), jnp.float32, least / len(cuts), top_value / len(cuts)))
        gain = gain * jnp.repeat(steps, shape[dim] // blocks).reshape([-1 if axis == dim else 1 for axis in range(len(shape))])
    return gain


def centred(rng, shape, scale, bound, cuts=(), held_as=jnp.bfloat16):
    gain = shard_levels(rng, shape, cuts, -0.22, 0.18) if cuts else 1.0
    entries = jax.random.normal(rng, shape, jnp.float32) * scale * gain
    return jnp.minimum(jnp.maximum(entries, -bound), bound).astype(held_as)


def setup_inputs(seed: int = 0) -> dict:
    keys = jax.random.split(jax.random.key(seed), 9)
    echo_data = centred(keys[0], (N_SLAB, CHAN, SAMPLES), 1.0, 6.0, ((0, 64), (1, 8)))
    acquirer = draw_acquirer(jax.random.fold_in(keys[8], 71), 0)
    panels = centred(keys[2], (N_SLAB, TX, NB, BLK, BLK), (BLK * CHAN * 16) ** -0.5, 0.00390625, ((0, 64), (2, 8)))
    block_count = draw_block_count(jax.random.fold_in(keys[8], 71), 0)
    block_rows = with_ends(jax.random.randint(keys[4], (N_SLAB, TX, NB), 0, RB), jax.random.fold_in(keys[4], 1), 0, RB - 1).astype(jnp.int32)
    block_columns = with_ends(jax.random.randint(keys[5], (N_SLAB, TX, NB), 0, SB), jax.random.fold_in(keys[5], 1), 0, SB - 1).astype(jnp.int32)
    apodization = jnp.clip(jnp.exp(math.log(2.5) - 2.3025851 * jax.random.uniform(keys[6], (NWIN, CHAN), jnp.float32) ** shard_levels(keys[6], (NWIN, CHAN), ((1, 8),), -0.2, 0.2)), 0.25, 2.5)
    window_index = with_ends(jax.random.randint(keys[7], (VOXELS,), 0, NWIN), jax.random.fold_in(keys[7], 1), 0, NWIN - 1).astype(jnp.int32)
    return dict(echo_data=echo_data, acquirer=acquirer, panels=panels, block_count=block_count, block_rows=block_rows, block_columns=block_columns, apodization=apodization, window_index=window_index)


def reference(echo_data, acquirer, panels, block_count, block_rows, block_columns, apodization, window_index):
    grids = [echo_data[acquirer[transmit]].reshape(CHAN, SB, BLK) for transmit in range(TX)]

    def slab_image(inputs):
        slab_panels, slab_counts, slab_rows, slab_columns, slab_windows = inputs
        running = jnp.zeros((RB, BLK, CHAN), jnp.float32)
        for transmit in range(TX):
            picked = jnp.take(grids[transmit], slab_columns[transmit].astype(jnp.int32), axis=1)
            terms = jnp.einsum("kvs,cks->kvc", slab_panels[transmit].astype(jnp.float32), picked.astype(jnp.float32))
            live = (jnp.arange(NB, dtype=jnp.int32) < slab_counts[transmit]).astype(jnp.float32)
            onehot = (slab_rows[transmit][:, None] == jnp.arange(RB, dtype=jnp.int32)[None, :]).astype(jnp.float32) * live[:, None]
            running = running + jnp.einsum("kr,kvc->rvc", onehot, terms, precision=lax.Precision.HIGHEST)
        weights = jnp.take(apodization, slab_windows.astype(jnp.int32), axis=0)
        return jnp.sum(running.reshape(VOX_SLAB, CHAN) * weights, axis=1)

    slabs = lax.map(slab_image, (panels, block_count, block_rows, block_columns, window_index.reshape(N_SLAB, VOX_SLAB)))
    return slabs.reshape(VOXELS)
```

```python
import jax
import jax.numpy as jnp
from jax import lax
from jax.experimental import pallas as pl
from jax.experimental.pallas import tpu as pltpu
from jax.sharding import PartitionSpec as P

LANES = 128
VMEM = pl.BlockSpec(memory_space=pltpu.VMEM)
SMEM = pl.BlockSpec(memory_space=pltpu.SMEM)
NT = (((1,), (1,)), ((), ()))
PARAMS = pltpu.CompilerParams(vmem_limit_bytes=8 * 1024 * 1024)


def window_sums(apodization, echo):
    windows, channels = apodization.shape
    samples = echo.shape[-1]
    blocks, quarters = samples // LANES, windows // 4

    def kernel(apod_ref, echo_ref, out_ref):
        apod = apod_ref[...]
        high = apod.astype(jnp.bfloat16)
        rest = apod - high.astype(jnp.float32)
        middle = rest.astype(jnp.bfloat16)
        low = (rest - middle.astype(jnp.float32)).astype(jnp.bfloat16)
        terms = jnp.concatenate([high, middle, low], axis=0)
        sums = jnp.dot(terms, echo_ref[0], preferred_element_type=jnp.float32)
        sums = sums[:windows] + (sums[windows : 2 * windows] + sums[2 * windows :])
        for block in range(blocks):
            for quarter in range(quarters):
                out_ref[block * quarters + quarter] = sums[
                    4 * quarter : 4 * quarter + 4, block * LANES : (block + 1) * LANES
                ]

    return pl.pallas_call(
        kernel,
        out_shape=jax.ShapeDtypeStruct((blocks * quarters, 4, LANES), jnp.float32),
        in_specs=[VMEM, VMEM],
        out_specs=VMEM,
        compiler_params=PARAMS,
    )(apodization, echo)


def pick_acquirers(acquirer, pieces, copies):
    transmits = acquirer.shape[0]

    def kernel(acquirer_ref, pieces_ref, out_ref):
        for transmit in range(transmits):
            picked = pieces_ref[acquirer_ref[transmit]]
            for copy in range(copies):
                out_ref[copy, transmit] = picked

    return pl.pallas_call(
        kernel,
        out_shape=jax.ShapeDtypeStruct((copies, transmits) + pieces.shape[1:], pieces.dtype),
        in_specs=[SMEM, VMEM],
        out_specs=VMEM,
        compiler_params=PARAMS,
    )(acquirer, pieces)


def sum_and_copy(parts, copies):
    def kernel(parts_ref, out_ref):
        total = jnp.sum(parts_ref[...], axis=0)
        for copy in range(copies):
            out_ref[copy] = total

    return pl.pallas_call(
        kernel,
        out_shape=jax.ShapeDtypeStruct((copies,) + parts.shape[1:], parts.dtype),
        in_specs=[VMEM],
        out_specs=VMEM,
        compiler_params=PARAMS,
    )(parts)


def slot_sums(counts, rows, columns, windows_of_voxels, table, panels):
    transmits, slots, block, _ = panels.shape[1:]
    quarters = 4
    row_blocks = windows_of_voxels.shape[0] // block
    windows = quarters * table.shape[2]
    windows_of_voxels = windows_of_voxels.reshape(row_blocks, 1, block)

    def kernel(counts_ref, rows_ref, columns_ref, index_ref, table_ref, panels_ref, out_ref, total):
        first = lax.axis_index("grp") * slots
        total[...] = jnp.zeros_like(total)
        for transmit in range(transmits):
            for slot in range(slots):
                k = first + slot
                column = columns_ref[0, transmit, k]
                row = jnp.where(k < counts_ref[0, transmit], rows_ref[0, transmit, k], row_blocks)
                weighted = jnp.concatenate(
                    [table_ref[column * quarters + quarter, transmit] for quarter in range(quarters)],
                    axis=0,
                )
                high = weighted.astype(jnp.bfloat16)
                low = (weighted - high.astype(jnp.float32)).astype(jnp.bfloat16)
                terms = lax.dot_general(
                    jnp.concatenate([high, low], axis=0),
                    panels_ref[0, transmit, slot],
                    NT,
                    preferred_element_type=jnp.float32,
                )
                total[row] += terms[:windows] + terms[windows:]
        number = lax.broadcasted_iota(jnp.int32, (windows, block), 0)
        for row in range(row_blocks):
            chosen = jnp.where(number == index_ref[row], total[row], 0.0)
            out_ref[row] = jnp.sum(chosen, axis=0, keepdims=True)

    return pl.pallas_call(
        kernel,
        out_shape=jax.ShapeDtypeStruct((row_blocks, 1, block), jnp.float32),
        in_specs=[SMEM, SMEM, SMEM, VMEM, VMEM, VMEM],
        out_specs=VMEM,
        compiler_params=PARAMS,
        scratch_shapes=[pltpu.VMEM((row_blocks + 1, windows, block), jnp.float32)],
    )(counts, rows, columns, windows_of_voxels, table, panels)


def exchange(pieces, axis):
    return lax.all_to_all(pieces, axis, split_axis=0, concat_axis=0, tiled=True)


def per_device(
    echo_data, acquirer, panels, block_count, block_rows, block_columns, apodization, window_index
):
    slabs, groups = lax.axis_size("slab"), lax.axis_size("grp")
    pieces = exchange(window_sums(apodization, echo_data), "slab")
    parts = exchange(pick_acquirers(acquirer, pieces, groups), "grp")
    table = exchange(sum_and_copy(parts, slabs), "slab")
    partial = slot_sums(block_count, block_rows, block_columns, window_index, table, panels)
    return jnp.sum(exchange(partial, "grp"), axis=(0, 1))


def solution(mesh):
    return jax.shard_map(
        per_device,
        mesh=mesh,
        in_specs=(
            P("slab", "grp", None),
            P(),
            P("slab", None, "grp", None, None),
            P("slab", None),
            P("slab", None, None),
            P("slab", None, None),
            P(None, "grp"),
            P("slab"),
        ),
        out_specs=P(("slab", "grp")),
        check_vma=False,
    )
```

```python
import jax
import jax.numpy as jnp
from jax import lax
from jax.experimental import pallas as pl
from jax.experimental.pallas import tpu as pltpu
from jax.sharding import PartitionSpec as P

LANES = 128
VMEM = pl.BlockSpec(memory_space=pltpu.VMEM)
SMEM = pl.BlockSpec(memory_space=pltpu.SMEM)
NT = (((1,), (1,)), ((), ()))
PARAMS = pltpu.CompilerParams(vmem_limit_bytes=8 * 1024 * 1024)


def window_sums(apodization, echo):
    windows, channels = apodization.shape
    samples = echo.shape[-1]
    blocks, quarters = samples // LANES, windows // 4

    def kernel(apod_ref, echo_ref, out_ref):
        apod = apod_ref[...]
        high = apod.astype(jnp.bfloat16)
        rest = apod - high.astype(jnp.float32)
        middle = rest.astype(jnp.bfloat16)
        low = (rest - middle.astype(jnp.float32)).astype(jnp.bfloat16)
        terms = jnp.concatenate([high, middle, low], axis=0)
        sums = jnp.dot(terms, echo_ref[0], preferred_element_type=jnp.float32)
        sums = sums[:windows] + (sums[windows : 2 * windows] + sums[2 * windows :])
        for block in range(blocks):
            for quarter in range(quarters):
                out_ref[block * quarters + quarter] = sums[
                    4 * quarter : 4 * quarter + 4, block * LANES : (block + 1) * LANES
                ]

    return pl.pallas_call(
        kernel,
        out_shape=jax.ShapeDtypeStruct((blocks * quarters, 4, LANES), jnp.float32),
        in_specs=[VMEM, VMEM],
        out_specs=VMEM,
        compiler_params=PARAMS,
    )(apodization, echo)


def pick_acquirers(acquirer, pieces, copies):
    transmits = acquirer.shape[0]

    def kernel(acquirer_ref, pieces_ref, out_ref):
        for transmit in range(transmits):
            picked = pieces_ref[acquirer_ref[transmit]]
            for copy in range(copies):
                out_ref[copy, transmit] = picked

    return pl.pallas_call(
        kernel,
        out_shape=jax.ShapeDtypeStruct((copies, transmits) + pieces.shape[1:], pieces.dtype),
        in_specs=[SMEM, VMEM],
        out_specs=VMEM,
        compiler_params=PARAMS,
    )(acquirer, pieces)


def sum_and_copy(parts, copies):
    def kernel(parts_ref, out_ref):
        total = jnp.sum(parts_ref[...], axis=0)
        for copy in range(copies):
            out_ref[copy] = total

    return pl.pallas_call(
        kernel,
        out_shape=jax.ShapeDtypeStruct((copies,) + parts.shape[1:], parts.dtype),
        in_specs=[VMEM],
        out_specs=VMEM,
        compiler_params=PARAMS,
    )(parts)


def slot_sums(counts, rows, columns, windows_of_voxels, table, panels):
    transmits, slots, block, _ = panels.shape[1:]
    quarters = 4
    row_blocks = windows_of_voxels.shape[0] // block
    windows = quarters * table.shape[2]
    windows_of_voxels = windows_of_voxels.reshape(row_blocks, 1, block)

    def kernel(counts_ref, rows_ref, columns_ref, index_ref, table_ref, panels_ref, out_ref, total):
        first = lax.axis_index("grp") * slots
        total[...] = jnp.zeros_like(total)
        for transmit in range(transmits):
            for slot in range(slots):
                k = first + slot
                column = columns_ref[transmit, 0, k]
                row = jnp.where(k < counts_ref[0, transmit], rows_ref[transmit, 0, k], row_blocks)
                weighted = jnp.concatenate(
                    [table_ref[column * quarters + quarter, transmit] for quarter in range(quarters)],
                    axis=0,
                )
                high = weighted.astype(jnp.bfloat16)
                low = (weighted - high.astype(jnp.float32)).astype(jnp.bfloat16)
                terms = lax.dot_general(
                    jnp.concatenate([high, low], axis=0),
                    panels_ref[0, transmit, slot],
                    NT,
                    preferred_element_type=jnp.float32,
                )
                total[row] += terms[:windows] + terms[windows:]
        number = lax.broadcasted_iota(jnp.int32, (windows, block), 0)
        for row in range(row_blocks):
            chosen = jnp.where(number == index_ref[row], total[row], 0.0)
            out_ref[row] = jnp.sum(chosen, axis=0, keepdims=True)

    return pl.pallas_call(
        kernel,
        out_shape=jax.ShapeDtypeStruct((row_blocks, 1, block), jnp.float32),
        in_specs=[SMEM, SMEM, SMEM, VMEM, VMEM, VMEM],
        out_specs=VMEM,
        compiler_params=PARAMS,
        scratch_shapes=[pltpu.VMEM((row_blocks + 1, windows, block), jnp.float32)],
    )(counts, rows, columns, windows_of_voxels, table, panels)


def exchange(pieces, axis):
    return lax.all_to_all(pieces, axis, split_axis=0, concat_axis=0, tiled=True)


def per_device(
    echo_data, acquirer, panels, block_count, block_rows, block_columns, apodization, window_index
):
    slabs, groups = lax.axis_size("slab"), lax.axis_size("grp")
    pieces = exchange(window_sums(apodization, echo_data), "slab")
    parts = exchange(pick_acquirers(acquirer, pieces, groups), "grp")
    table = exchange(sum_and_copy(parts, slabs), "slab")
    rows, columns = (jnp.transpose(x, (1, 0, 2)) for x in (block_rows, block_columns))
    partial = slot_sums(block_count, rows, columns, window_index, table, panels)
    return jnp.sum(exchange(partial, "grp"), axis=(0, 1))


def solution(mesh):
    return jax.shard_map(
        per_device,
        mesh=mesh,
        in_specs=(
            P("slab", "grp", None),
            P(),
            P("slab", None, "grp", None, None),
            P("slab", None),
            P("slab", None, None),
            P("slab", None, None),
            P(None, "grp"),
            P("slab"),
        ),
        out_specs=P(("slab", "grp")),
        check_vma=False,
    )
```

```python
import jax
import jax.numpy as jnp
from jax import lax
from jax.experimental import pallas as pl
from jax.experimental.pallas import tpu as pltpu
from jax.sharding import PartitionSpec as P

LANES = 128
Y, Z = 8, 2
VMEM = pl.BlockSpec(memory_space=pltpu.VMEM)
SMEM = pl.BlockSpec(memory_space=pltpu.SMEM)
NT = (((1,), (1,)), ((), ()))
PARAMS = pltpu.CompilerParams(vmem_limit_bytes=8 * 1024 * 1024)


def swap_granules(arrays):
    arrays = list(arrays)
    count = len(arrays)
    width = LANES // count
    granule = lax.broadcasted_iota(jnp.int32, arrays[0].shape, 1) // width
    step = count // 2
    while step:
        upper = (granule & step) != 0
        for low in range(count):
            if low & step:
                continue
            a, b = arrays[low], arrays[low + step]
            arrays[low] = jnp.where(upper, pltpu.roll(b, step * width, 1), a)
            arrays[low + step] = jnp.where(upper, b, pltpu.roll(a, LANES - step * width, 1))
        step //= 2
    return arrays


def window_sums(apodization, echo, groups):
    windows, channels = apodization.shape
    samples = echo.shape[-1]
    halves = samples // LANES // groups

    def kernel(apod_ref, echo_ref, out_ref):
        apod = apod_ref[...]
        high = apod.astype(jnp.bfloat16)
        rest = apod - high.astype(jnp.float32)
        middle = rest.astype(jnp.bfloat16)
        low = (rest - middle.astype(jnp.float32)).astype(jnp.bfloat16)
        terms = jnp.concatenate([high, middle, low], axis=0)
        sums = jnp.dot(terms, echo_ref[0], preferred_element_type=jnp.float32)
        sums = sums[:windows] + (sums[windows : 2 * windows] + sums[2 * windows :])
        for half in range(halves):
            blocks = [
                sums[:, (half * groups + i) * LANES : (half * groups + i + 1) * LANES]
                for i in range(groups)
            ]
            for group, share in enumerate(swap_granules(blocks)):
                out_ref[group, half] = share

    return pl.pallas_call(
        kernel,
        out_shape=jax.ShapeDtypeStruct((groups, halves, windows, LANES), jnp.float32),
        in_specs=[VMEM, VMEM],
        out_specs=VMEM,
        compiler_params=PARAMS,
    )(apodization, echo)


def panel_shares(panels, groups):
    transmits, slots, block, _ = panels.shape[1:]

    def kernel(panels_ref, out_ref):
        for transmit in range(transmits):
            for start in range(0, block, 32):
                rows = pl.ds(start, 32)
                tiles = [panels_ref[0, transmit, slot, rows].astype(jnp.float32) for slot in range(slots)]
                for group, share in enumerate(swap_granules(tiles)):
                    out_ref[group, transmit, rows] = share.astype(jnp.bfloat16)

    return pl.pallas_call(
        kernel,
        out_shape=jax.ShapeDtypeStruct((groups, transmits, block, LANES), panels.dtype),
        in_specs=[VMEM],
        out_specs=VMEM,
        compiler_params=PARAMS,
    )(panels)


def sum_and_copy(parts, copies):
    def kernel(parts_ref, out_ref):
        total = jnp.sum(parts_ref[...], axis=0)
        for copy in range(copies):
            out_ref[copy] = total

    return pl.pallas_call(
        kernel,
        out_shape=jax.ShapeDtypeStruct((copies,) + parts.shape[1:], parts.dtype),
        in_specs=[VMEM],
        out_specs=VMEM,
        compiler_params=PARAMS,
    )(parts)


def pick_and_copy(acquirer, line, copies):
    transmits = acquirer.shape[0]

    def kernel(acquirer_ref, line_ref, out_ref):
        for transmit in range(transmits):
            picked = line_ref[lax.rem(lax.div(acquirer_ref[transmit], Z), Y)]
            for copy in range(copies):
                out_ref[copy, transmit] = picked

    return pl.pallas_call(
        kernel,
        out_shape=jax.ShapeDtypeStruct((copies, transmits) + line.shape[1:], line.dtype),
        in_specs=[SMEM, VMEM],
        out_specs=VMEM,
        compiler_params=PARAMS,
    )(acquirer, line)


def slot_sums(acquirer, counts, rows, columns, windows_of_voxels, table, shares):
    groups, transmits, block, _ = shares.shape
    windows = table.shape[3]
    slots = rows.shape[2] // groups
    width = LANES // slots
    row_blocks = windows_of_voxels.shape[0] // block
    windows_of_voxels = windows_of_voxels.reshape(row_blocks, 1, block)

    def kernel(acquirer_ref, counts_ref, rows_ref, columns_ref, index_ref, table_ref, shares_ref, out_ref):
        granule = lax.broadcasted_iota(jnp.int32, (windows, LANES), 1) // width
        total = jnp.zeros((row_blocks * 2 * windows, block), jnp.float32)
        for transmit in range(transmits):
            root = acquirer_ref[transmit]
            member = lax.div(root, Y * Z) * Z + lax.rem(root, Z)
            for group in range(groups):
                gathered = jnp.zeros((windows, LANES), jnp.float32)
                row_of = jnp.full((windows, LANES), row_blocks, jnp.int32)
                for i in range(slots):
                    k = group * slots + i
                    column = columns_ref[transmit, 0, k]
                    row = jnp.where(k < counts_ref[0, transmit], rows_ref[transmit, 0, k], row_blocks)
                    samples = table_ref[member, transmit, lax.div(column, slots)]
                    samples = pltpu.roll(samples, ((i - column) & (slots - 1)) * width, 1)
                    gathered = jnp.where(granule == i, samples, gathered)
                    row_of = jnp.where(granule == i, row, row_of)
                high = gathered.astype(jnp.bfloat16).astype(jnp.float32)
                low = gathered - high
                left = []
                for row in range(row_blocks):
                    left.append(jnp.where(row_of == row, high, 0.0).astype(jnp.bfloat16))
                    left.append(jnp.where(row_of == row, low, 0.0).astype(jnp.bfloat16))
                total += lax.dot_general(
                    jnp.concatenate(left, axis=0),
                    shares_ref[group, transmit],
                    NT,
                    preferred_element_type=jnp.float32,
                )
        number = lax.broadcasted_iota(jnp.int32, (windows, block), 0)
        for row in range(row_blocks):
            start = 2 * windows * row
            both = total[start : start + windows] + total[start + windows : start + 2 * windows]
            out_ref[row] = jnp.sum(jnp.where(number == index_ref[row], both, 0.0), axis=0, keepdims=True)

    return pl.pallas_call(
        kernel,
        out_shape=jax.ShapeDtypeStruct((row_blocks, 1, block), jnp.float32),
        in_specs=[SMEM, SMEM, SMEM, SMEM, VMEM, VMEM, VMEM],
        out_specs=VMEM,
        compiler_params=PARAMS,
    )(acquirer, counts, rows, columns, windows_of_voxels, table, shares)


def exchange(pieces, axis, lines=None):
    return lax.all_to_all(
        pieces, axis, split_axis=0, concat_axis=0, axis_index_groups=lines, tiled=True
    )


def per_device(
    echo_data, acquirer, panels, block_count, block_rows, block_columns, apodization, window_index
):
    slabs, groups = lax.axis_size("slab"), lax.axis_size("grp")
    x = slabs // (Y * Z)
    along_y = [[(i * Y + j) * Z + k for j in range(Y)] for i in range(x) for k in range(Z)]
    along_xz = [[(i * Y + j) * Z + k for i in range(x) for k in range(Z)] for j in range(Y)]
    shares = exchange(panel_shares(panels, groups), "grp")
    parts = exchange(window_sums(apodization, echo_data, groups), "grp")
    line = lax.all_gather(sum_and_copy(parts, 1)[0], "slab", axis_index_groups=along_y)
    table = lax.all_gather(pick_and_copy(acquirer, line, 1)[0], "slab", axis_index_groups=along_xz)
    rows, columns = (jnp.transpose(v, (1, 0, 2)) for v in (block_rows, block_columns))
    partial = slot_sums(acquirer, block_count, rows, columns, window_index, table, shares)
    return jnp.sum(exchange(partial, "grp"), axis=(0, 1))


def solution(mesh):
    return jax.shard_map(
        per_device,
        mesh=mesh,
        in_specs=(
            P("slab", "grp", None),
            P(),
            P("slab", None, "grp", None, None),
            P("slab", None),
            P("slab", None, None),
            P("slab", None, None),
            P(None, "grp"),
            P("slab"),
        ),
        out_specs=P(("slab", "grp")),
        check_vma=False,
    )
```

```python
import jax
import jax.numpy as jnp
from jax import lax
from jax.experimental import pallas as pl
from jax.experimental.pallas import tpu as pltpu
from jax.sharding import PartitionSpec as P

LANES, SUBLANES = 128, 8
Z = 2
VMEM = pl.BlockSpec(memory_space=pltpu.VMEM)
SMEM = pl.BlockSpec(memory_space=pltpu.SMEM)
NT = (((1,), (1,)), ((), ()))
PARAMS = pltpu.CompilerParams(vmem_limit_bytes=8 * 1024 * 1024)


def window_sums(apodization, echo):
    windows, channels = apodization.shape
    samples = echo.shape[-1]
    blocks, halves = samples // LANES, windows // SUBLANES

    def kernel(apod_ref, echo_ref, out_ref):
        apod = apod_ref[...]
        high = apod.astype(jnp.bfloat16)
        rest = apod - high.astype(jnp.float32)
        middle = rest.astype(jnp.bfloat16)
        low = (rest - middle.astype(jnp.float32)).astype(jnp.bfloat16)
        terms = jnp.concatenate([high, middle, low], axis=0)
        sums = jnp.dot(terms, echo_ref[0], preferred_element_type=jnp.float32)
        sums = sums[:windows] + (sums[windows : 2 * windows] + sums[2 * windows :])
        for block in range(blocks):
            for half in range(halves):
                out_ref[block * halves + half] = sums[
                    half * SUBLANES : (half + 1) * SUBLANES, block * LANES : (block + 1) * LANES
                ]

    return pl.pallas_call(
        kernel,
        out_shape=jax.ShapeDtypeStruct((blocks * halves, SUBLANES, LANES), jnp.float32),
        in_specs=[VMEM, VMEM],
        out_specs=VMEM,
        compiler_params=PARAMS,
    )(apodization, echo)


def pick_acquirers(acquirer, pieces, copies, rows, slots):
    transmits = acquirer.shape[0]

    def kernel(acquirer_ref, pieces_ref, rows_ref, out_ref, rows_out):
        for transmit in range(transmits):
            picked = pieces_ref[lax.div(acquirer_ref[transmit], Z)]
            for copy in range(copies):
                out_ref[copy, transmit] = picked
        first = lax.axis_index("grp") * slots
        for transmit in range(transmits):
            for slot in range(slots):
                rows_out[transmit * slots + slot] = rows_ref[transmit, 0, first + slot]

    return pl.pallas_call(
        kernel,
        out_shape=(
            jax.ShapeDtypeStruct((copies, transmits) + pieces.shape[1:], pieces.dtype),
            jax.ShapeDtypeStruct((transmits * slots,), jnp.int32),
        ),
        in_specs=[SMEM, VMEM, SMEM],
        out_specs=(VMEM, SMEM),
        compiler_params=PARAMS,
    )(acquirer, pieces, rows)


def sum_and_copy(acquirer, parts, groups, copies, counts, own_rows, columns, slots, row_blocks):
    transmits = acquirer.shape[0]

    def kernel(acquirer_ref, parts_ref, counts_ref, rows_ref, columns_ref, out_ref, slots_out):
        for transmit in range(transmits):
            start = lax.rem(acquirer_ref[transmit], Z) * groups
            total = parts_ref[start, transmit]
            for group in range(1, groups):
                total += parts_ref[start + group, transmit]
            for copy in range(copies):
                out_ref[copy, transmit] = total
        first = lax.axis_index("grp") * slots
        for transmit in range(transmits):
            for slot in range(slots):
                place, k = transmit * slots + slot, first + slot
                live = k < counts_ref[0, transmit]
                slots_out[0, place] = jnp.where(live, rows_ref[place], row_blocks)
                slots_out[1, place] = columns_ref[transmit, 0, k]

    return pl.pallas_call(
        kernel,
        out_shape=(
            jax.ShapeDtypeStruct((copies,) + parts.shape[1:], parts.dtype),
            jax.ShapeDtypeStruct((2, transmits * slots), jnp.int32),
        ),
        in_specs=[SMEM, VMEM, SMEM, SMEM, SMEM],
        out_specs=(VMEM, SMEM),
        compiler_params=PARAMS,
    )(acquirer, parts, counts, own_rows, columns)


def slot_sums(slot_table, windows_of_voxels, table, panels, halves):
    transmits, slots, block, _ = panels.shape[1:]
    row_blocks = windows_of_voxels.shape[0]
    windows = halves * SUBLANES

    def kernel(slots_ref, index_ref, table_ref, panels_ref, out_ref, total):
        total[...] = jnp.zeros_like(total)
        for transmit in range(transmits):
            for slot in range(slots):
                row = slots_ref[0, transmit * slots + slot]
                column = slots_ref[1, transmit * slots + slot]
                weighted = jnp.concatenate(
                    [table_ref[column * halves + half, transmit] for half in range(halves)], axis=0
                )
                high = weighted.astype(jnp.bfloat16)
                low = (weighted - high.astype(jnp.float32)).astype(jnp.bfloat16)
                terms = lax.dot_general(
                    jnp.concatenate([high, low], axis=0),
                    panels_ref[0, transmit, slot],
                    NT,
                    preferred_element_type=jnp.float32,
                )
                total[row] += terms[:windows] + terms[windows:]
        number = lax.broadcasted_iota(jnp.int32, (windows, block), 0)
        for row in range(row_blocks):
            chosen = jnp.where(number == index_ref[row], total[row], 0.0)
            out_ref[row] = jnp.sum(chosen, axis=0, keepdims=True)

    return pl.pallas_call(
        kernel,
        out_shape=jax.ShapeDtypeStruct((row_blocks, 1, block), jnp.float32),
        in_specs=[SMEM, VMEM, VMEM, VMEM],
        out_specs=VMEM,
        scratch_shapes=[pltpu.VMEM((row_blocks + 1, windows, block), jnp.float32)],
        compiler_params=PARAMS,
    )(slot_table, windows_of_voxels, table, panels)


def exchange(pieces, axis, lines=None):
    return lax.all_to_all(
        pieces, axis, split_axis=0, concat_axis=0, axis_index_groups=lines, tiled=True
    )


def per_device(
    echo_data, acquirer, panels, block_count, block_rows, block_columns, apodization, window_index
):
    slabs, groups = lax.axis_size("slab"), lax.axis_size("grp")
    slots, block = panels.shape[2], panels.shape[3]
    planes = [list(range(z, slabs, Z)) for z in range(Z)]
    lines = [
        [(chip * Z + z) * groups + group for z in range(Z) for group in range(groups)]
        for chip in range(slabs // Z)
    ]
    row_blocks = window_index.shape[0] // block
    rows, columns = (jnp.transpose(v, (1, 0, 2)) for v in (block_rows, block_columns))
    voxels = window_index.reshape(row_blocks, 1, block)
    pieces = exchange(window_sums(apodization, echo_data), "slab", planes)
    picked, own_rows = pick_acquirers(acquirer, pieces, Z * groups, rows, slots)
    parts = exchange(picked, ("slab", "grp"), lines)
    sums, slot_table = sum_and_copy(
        acquirer, parts, groups, slabs // Z, block_count, own_rows, columns, slots, row_blocks
    )
    table = exchange(sums, "slab", planes)
    partial = slot_sums(slot_table, voxels, table, panels, apodization.shape[0] // SUBLANES)
    return jnp.sum(exchange(partial, "grp"), axis=(0, 1))


def solution(mesh):
    return jax.shard_map(
        per_device,
        mesh=mesh,
        in_specs=(
            P("slab", "grp", None),
            P(),
            P("slab", None, "grp", None, None),
            P("slab", None),
            P("slab", None, None),
            P("slab", None, None),
            P(None, "grp"),
            P("slab"),
        ),
        out_specs=P(("slab", "grp")),
        check_vma=False,
    )
```

```python
import jax
import jax.numpy as jnp
from jax import lax
from jax.experimental import pallas as pl
from jax.experimental.pallas import tpu as pltpu
from jax.sharding import PartitionSpec as P

LANES = 128
VMEM = pl.BlockSpec(memory_space=pltpu.VMEM)
SMEM = pl.BlockSpec(memory_space=pltpu.SMEM)
NT = (((1,), (1,)), ((), ()))
PARAMS = pltpu.CompilerParams(vmem_limit_bytes=8 * 1024 * 1024)


def window_sums(apodization, echo):
    windows, channels = apodization.shape
    samples = echo.shape[-1]
    blocks, quarters = samples // LANES, windows // 4

    def kernel(apod_ref, echo_ref, out_ref):
        apod = apod_ref[...]
        high = apod.astype(jnp.bfloat16)
        rest = apod - high.astype(jnp.float32)
        middle = rest.astype(jnp.bfloat16)
        low = (rest - middle.astype(jnp.float32)).astype(jnp.bfloat16)
        terms = jnp.concatenate([high, middle, low], axis=0)
        sums = jnp.dot(terms, echo_ref[0], preferred_element_type=jnp.float32)
        sums = sums[:windows] + (sums[windows : 2 * windows] + sums[2 * windows :])
        for block in range(blocks):
            for quarter in range(quarters):
                out_ref[block * quarters + quarter] = sums[
                    4 * quarter : 4 * quarter + 4, block * LANES : (block + 1) * LANES
                ]

    return pl.pallas_call(
        kernel,
        out_shape=jax.ShapeDtypeStruct((blocks * quarters, 4, LANES), jnp.float32),
        in_specs=[VMEM, VMEM],
        out_specs=VMEM,
        compiler_params=PARAMS,
    )(apodization, echo)


def hand_on(refs, count):
    for i in range(count):
        refs[count + 1 + i][...] = refs[i][...]
    return refs[count]


def pick_acquirers(acquirer, pieces, copies, handed):
    transmits = acquirer.shape[0]

    def kernel(acquirer_ref, pieces_ref, *refs):
        out_ref = hand_on(refs, len(handed))
        for transmit in range(transmits):
            picked = pieces_ref[acquirer_ref[transmit]]
            for copy in range(copies):
                out_ref[copy, transmit] = picked

    return pl.pallas_call(
        kernel,
        out_shape=(
            jax.ShapeDtypeStruct((copies, transmits) + pieces.shape[1:], pieces.dtype),
            *(jax.ShapeDtypeStruct(table.shape, table.dtype) for table in handed),
        ),
        in_specs=[SMEM, VMEM] + [VMEM] * len(handed),
        out_specs=(VMEM,) * (1 + len(handed)),
        compiler_params=PARAMS,
    )(acquirer, pieces, *handed)


def sum_and_copy(parts, copies, handed):
    def kernel(parts_ref, *refs):
        out_ref = hand_on(refs, len(handed))
        total = jnp.sum(parts_ref[...], axis=0)
        for copy in range(copies):
            out_ref[copy] = total

    return pl.pallas_call(
        kernel,
        out_shape=(
            jax.ShapeDtypeStruct((copies,) + parts.shape[1:], parts.dtype),
            *(jax.ShapeDtypeStruct(table.shape, table.dtype) for table in handed),
        ),
        in_specs=[VMEM] * (1 + len(handed)),
        out_specs=(VMEM,) * (1 + len(handed)),
        compiler_params=PARAMS,
    )(parts, *handed)


def slot_sums(counts, rows, columns, windows_of_voxels, table, panels):
    transmits, slots, block, _ = panels.shape[1:]
    quarters = 4
    row_blocks = windows_of_voxels.shape[0]
    windows = quarters * table.shape[2]

    def kernel(counts_ref, rows_ref, columns_ref, index_ref, table_ref, panels_ref, out_ref, total):
        first = lax.axis_index("grp") * slots
        total[...] = jnp.zeros_like(total)
        for transmit in range(transmits):
            for slot in range(slots):
                k = first + slot
                column = columns_ref[transmit, 0, k]
                row = jnp.where(k < counts_ref[0, transmit], rows_ref[transmit, 0, k], row_blocks)
                weighted = jnp.concatenate(
                    [table_ref[column * quarters + quarter, transmit] for quarter in range(quarters)],
                    axis=0,
                )
                high = weighted.astype(jnp.bfloat16)
                low = (weighted - high.astype(jnp.float32)).astype(jnp.bfloat16)
                terms = lax.dot_general(
                    jnp.concatenate([high, low], axis=0),
                    panels_ref[0, transmit, slot],
                    NT,
                    preferred_element_type=jnp.float32,
                )
                total[row] += terms[:windows] + terms[windows:]
        number = lax.broadcasted_iota(jnp.int32, (windows, block), 0)
        for row in range(row_blocks):
            chosen = jnp.where(number == index_ref[row], total[row], 0.0)
            out_ref[row] = jnp.sum(chosen, axis=0, keepdims=True)

    return pl.pallas_call(
        kernel,
        out_shape=jax.ShapeDtypeStruct((row_blocks, 1, block), jnp.float32),
        in_specs=[SMEM, SMEM, SMEM, VMEM, VMEM, VMEM],
        out_specs=VMEM,
        compiler_params=PARAMS,
        scratch_shapes=[pltpu.VMEM((row_blocks + 1, windows, block), jnp.float32)],
    )(counts, rows, columns, windows_of_voxels, table, panels)


def exchange(pieces, axis):
    return lax.all_to_all(pieces, axis, split_axis=0, concat_axis=0, tiled=True)


def per_device(
    echo_data, acquirer, panels, block_count, block_rows, block_columns, apodization, window_index
):
    slabs, groups = lax.axis_size("slab"), lax.axis_size("grp")
    rows, columns = (jnp.transpose(x, (1, 0, 2)) for x in (block_rows, block_columns))
    pieces = exchange(window_sums(apodization, echo_data), "slab")
    voxels = window_index.reshape(-1, 1, panels.shape[-1])
    picked, rows, voxels = pick_acquirers(acquirer, pieces, groups, (rows, voxels))
    sums, columns, counts = sum_and_copy(exchange(picked, "grp"), slabs, (columns, block_count))
    table = exchange(sums, "slab")
    partial = slot_sums(counts, rows, columns, voxels, table, panels)
    return jnp.sum(exchange(partial, "grp"), axis=(0, 1))


def solution(mesh):
    return jax.shard_map(
        per_device,
        mesh=mesh,
        in_specs=(
            P("slab", "grp", None),
            P(),
            P("slab", None, "grp", None, None),
            P("slab", None),
            P("slab", None, None),
            P("slab", None, None),
            P(None, "grp"),
            P("slab"),
        ),
        out_specs=P(("slab", "grp")),
        check_vma=False,
    )
```

```python
import jax
import jax.numpy as jnp
from jax import lax
from jax.experimental import pallas as pl
from jax.experimental.pallas import tpu as pltpu
from jax.sharding import PartitionSpec as P

LANES = 128
Z = 2
VMEM = pl.BlockSpec(memory_space=pltpu.VMEM)
SMEM = pl.BlockSpec(memory_space=pltpu.SMEM)
NT = (((1,), (1,)), ((), ()))
PARAMS = pltpu.CompilerParams(vmem_limit_bytes=8 * 1024 * 1024)


def window_sums(apodization, echo):
    windows, channels = apodization.shape
    samples = echo.shape[-1]
    pairs, quarters = samples // (2 * LANES), windows // 4

    def kernel(apod_ref, echo_ref, out_ref):
        apod = apod_ref[...]
        high = apod.astype(jnp.bfloat16)
        rest = apod - high.astype(jnp.float32)
        middle = rest.astype(jnp.bfloat16)
        low = (rest - middle.astype(jnp.float32)).astype(jnp.bfloat16)
        terms = jnp.concatenate([high, middle, low], axis=0)
        sums = jnp.dot(terms, echo_ref[0], preferred_element_type=jnp.float32)
        sums = sums[:windows] + (sums[windows : 2 * windows] + sums[2 * windows :])
        left = lax.broadcasted_iota(jnp.int32, (windows, LANES), 1) < LANES // 2
        for pair in range(pairs):
            first, second = (
                sums[:, (2 * pair + i) * LANES : (2 * pair + i + 1) * LANES] for i in range(2)
            )
            halves = (
                jnp.where(left, first, pltpu.roll(second, LANES // 2, 1)),
                jnp.where(left, pltpu.roll(first, LANES // 2, 1), second),
            )
            for quarter in range(quarters):
                for half in range(2):
                    out_ref[pair * quarters + quarter, half] = halves[half][4 * quarter : 4 * quarter + 4]

    return pl.pallas_call(
        kernel,
        out_shape=jax.ShapeDtypeStruct((pairs * quarters, 2, 4, LANES), jnp.float32),
        in_specs=[VMEM, VMEM],
        out_specs=VMEM,
        compiler_params=PARAMS,
    )(apodization, echo)


def hand_on(refs, count):
    for i in range(count):
        refs[count + 1 + i][...] = refs[i][...]
    return refs[count]


def pick_acquirers(acquirer, pieces, copies, handed):
    transmits = acquirer.shape[0]

    def kernel(acquirer_ref, pieces_ref, *refs):
        out_ref = hand_on(refs, len(handed))
        for transmit in range(transmits):
            for half in range(2):
                picked = pieces_ref[lax.div(acquirer_ref[transmit], Z), half]
                for copy in range(half, copies, 2):
                    out_ref[copy, transmit] = picked

    return pl.pallas_call(
        kernel,
        out_shape=(
            jax.ShapeDtypeStruct((copies, transmits) + pieces.shape[2:], pieces.dtype),
            *(jax.ShapeDtypeStruct(table.shape, table.dtype) for table in handed),
        ),
        in_specs=[SMEM, VMEM] + [VMEM] * len(handed),
        out_specs=(VMEM,) * (1 + len(handed)),
        compiler_params=PARAMS,
    )(acquirer, pieces, *handed)


def sum_and_copy(acquirer, parts, groups, copies, handed):
    transmits = acquirer.shape[0]

    def kernel(acquirer_ref, parts_ref, *refs):
        out_ref = hand_on(refs, len(handed))
        for transmit in range(transmits):
            start = lax.rem(acquirer_ref[transmit], Z) * groups
            total = parts_ref[start, transmit]
            for group in range(1, groups):
                total += parts_ref[start + group, transmit]
            for copy in range(copies):
                out_ref[copy, transmit] = total

    return pl.pallas_call(
        kernel,
        out_shape=(
            jax.ShapeDtypeStruct((copies,) + parts.shape[1:], parts.dtype),
            *(jax.ShapeDtypeStruct(table.shape, table.dtype) for table in handed),
        ),
        in_specs=[SMEM] + [VMEM] * (1 + len(handed)),
        out_specs=(VMEM,) * (1 + len(handed)),
        compiler_params=PARAMS,
    )(acquirer, parts, *handed)


def slot_sums(counts, rows, columns, windows_of_voxels, table, panels, others):
    transmits, slots, block, _ = panels.shape[1:]
    quarters = 4
    row_blocks = windows_of_voxels.shape[0]
    windows = quarters * table.shape[2]
    pairs = table.shape[0] // quarters

    def kernel(
        counts_ref, rows_ref, columns_ref, index_ref, table_ref, panels_ref, others_ref, out_ref, weights, total
    ):
        group = lax.axis_index("grp")
        core = group & 1
        mine = (lax.broadcasted_iota(jnp.int32, (windows, LANES), 1) // (LANES // 2)) == core
        for transmit in range(transmits):
            for pair in range(pairs):
                both = jnp.concatenate(
                    [table_ref[pair * quarters + quarter, transmit] for quarter in range(quarters)], axis=0
                )
                for i, aligned in enumerate((both, pltpu.roll(both, LANES // 2, 1))):
                    aligned = jnp.where(mine, aligned, 0.0)
                    high = aligned.astype(jnp.bfloat16)
                    low = (aligned - high.astype(jnp.float32)).astype(jnp.bfloat16)
                    weights[(transmit * pairs + pair) * 2 + i] = jnp.concatenate([high, low], axis=0)
        total[...] = jnp.zeros_like(total)
        for first, source_ref in ((group * slots, panels_ref), ((group ^ 1) * slots, others_ref)):
            for transmit in range(transmits):
                for slot in range(slots):
                    k = first + slot
                    column = columns_ref[transmit, 0, k]
                    row = jnp.where(k < counts_ref[0, transmit], rows_ref[transmit, 0, k], row_blocks)
                    terms = lax.dot_general(
                        weights[transmit * pairs * 2 + (column ^ core)],
                        source_ref[0, transmit, slot],
                        NT,
                        preferred_element_type=jnp.float32,
                    )
                    total[row] += terms[:windows] + terms[windows:]
        number = lax.broadcasted_iota(jnp.int32, (windows, block), 0)
        for row in range(row_blocks):
            chosen = jnp.where(number == index_ref[row], total[row], 0.0)
            out_ref[row] = jnp.sum(chosen, axis=0, keepdims=True)

    return pl.pallas_call(
        kernel,
        out_shape=jax.ShapeDtypeStruct((row_blocks, 1, block), jnp.float32),
        in_specs=[SMEM, SMEM, SMEM, VMEM, VMEM, VMEM, VMEM],
        out_specs=VMEM,
        scratch_shapes=[
            pltpu.VMEM((transmits * pairs * 2, 2 * windows, LANES), jnp.bfloat16),
            pltpu.VMEM((row_blocks + 1, windows, block), jnp.float32),
        ],
        compiler_params=PARAMS,
    )(counts, rows, columns, windows_of_voxels, table, panels, others)


def exchange(pieces, axis, lines=None):
    return lax.all_to_all(
        pieces, axis, split_axis=0, concat_axis=0, axis_index_groups=lines, tiled=True
    )


def per_device(
    echo_data, acquirer, panels, block_count, block_rows, block_columns, apodization, window_index
):
    slabs, groups = lax.axis_size("slab"), lax.axis_size("grp")
    planes = [list(range(z, slabs, Z)) for z in range(Z)]
    lines = [
        [(chip * Z + z) * groups + group for z in range(Z) for group in range(groups)]
        for chip in range(slabs // Z)
    ]
    rows, columns = (jnp.transpose(x, (1, 0, 2)) for x in (block_rows, block_columns))
    voxels = window_index.reshape(-1, 1, panels.shape[-1])
    sums, given = lax.optimization_barrier((window_sums(apodization, echo_data), panels))
    others = lax.ppermute(given, "grp", [(i, i ^ 1) for i in range(groups)])
    pieces = exchange(sums, "slab", planes)
    picked, rows = pick_acquirers(acquirer, pieces, Z * groups, (rows,))
    parts = exchange(picked, ("slab", "grp"), lines)
    sums, columns, counts = sum_and_copy(acquirer, parts, groups, slabs // Z, (columns, block_count))
    table = exchange(sums, "slab", planes)
    partial = slot_sums(counts, rows, columns, voxels, table, panels, others)
    return jnp.sum(exchange(partial, "grp"), axis=(0, 1))


def solution(mesh):
    return jax.shard_map(
        per_device,
        mesh=mesh,
        in_specs=(
            P("slab", "grp", None),
            P(),
            P("slab", None, "grp", None, None),
            P("slab", None),
            P("slab", None, None),
            P("slab", None, None),
            P(None, "grp"),
            P("slab"),
        ),
        out_specs=P(("slab", "grp")),
        check_vma=False,
    )
```

```python
import jax
import jax.numpy as jnp
from jax import lax
from jax.experimental import pallas as pl
from jax.experimental.pallas import tpu as pltpu
from jax.sharding import PartitionSpec as P

LANES = 128
COLUMN_BITS = 4
Z = 2
VMEM = pl.BlockSpec(memory_space=pltpu.VMEM)
SMEM = pl.BlockSpec(memory_space=pltpu.SMEM)
NT = (((1,), (1,)), ((), ()))
PARAMS = pltpu.CompilerParams(vmem_limit_bytes=8 * 1024 * 1024)


def window_sums(apodization, echo):
    windows, channels = apodization.shape
    samples = echo.shape[-1]
    pairs, quarters = samples // (2 * LANES), windows // 4

    def kernel(apod_ref, echo_ref, out_ref):
        apod = apod_ref[...]
        high = apod.astype(jnp.bfloat16)
        rest = apod - high.astype(jnp.float32)
        middle = rest.astype(jnp.bfloat16)
        low = (rest - middle.astype(jnp.float32)).astype(jnp.bfloat16)
        terms = jnp.concatenate([high, middle, low], axis=0)
        sums = jnp.dot(terms, echo_ref[0], preferred_element_type=jnp.float32)
        sums = sums[:windows] + (sums[windows : 2 * windows] + sums[2 * windows :])
        left = lax.broadcasted_iota(jnp.int32, (windows, LANES), 1) < LANES // 2
        for pair in range(pairs):
            first, second = (
                sums[:, (2 * pair + i) * LANES : (2 * pair + i + 1) * LANES] for i in range(2)
            )
            halves = (
                jnp.where(left, first, pltpu.roll(second, LANES // 2, 1)),
                jnp.where(left, pltpu.roll(first, LANES // 2, 1), second),
            )
            for quarter in range(quarters):
                for half in range(2):
                    out_ref[pair * quarters + quarter, half] = halves[half][4 * quarter : 4 * quarter + 4]

    return pl.pallas_call(
        kernel,
        out_shape=jax.ShapeDtypeStruct((pairs * quarters, 2, 4, LANES), jnp.float32),
        in_specs=[VMEM, VMEM],
        out_specs=VMEM,
        compiler_params=PARAMS,
    )(apodization, echo)


def pick_acquirers(acquirer, pieces, copies):
    transmits = acquirer.shape[0]

    def kernel(acquirer_ref, pieces_ref, out_ref):
        for transmit in range(transmits):
            for half in range(2):
                picked = pieces_ref[lax.div(acquirer_ref[transmit], Z), half]
                for copy in range(half, copies, 2):
                    out_ref[copy, transmit] = picked

    return pl.pallas_call(
        kernel,
        out_shape=jax.ShapeDtypeStruct((copies, transmits) + pieces.shape[2:], pieces.dtype),
        in_specs=[SMEM, VMEM],
        out_specs=VMEM,
        compiler_params=PARAMS,
    )(acquirer, pieces)


def sum_and_copy(acquirer, parts, groups, copies):
    transmits = acquirer.shape[0]

    def kernel(acquirer_ref, parts_ref, out_ref):
        for transmit in range(transmits):
            start = lax.rem(acquirer_ref[transmit], Z) * groups
            total = parts_ref[start, transmit]
            for group in range(1, groups):
                total += parts_ref[start + group, transmit]
            for copy in range(copies):
                out_ref[copy, transmit] = total

    return pl.pallas_call(
        kernel,
        out_shape=jax.ShapeDtypeStruct((copies,) + parts.shape[1:], parts.dtype),
        in_specs=[SMEM, VMEM],
        out_specs=VMEM,
        compiler_params=PARAMS,
    )(acquirer, parts)


def slot_sums(slot_table, windows_of_voxels, table, panels, others):
    transmits, slots, block, _ = panels.shape[1:]
    quarters = 4
    row_blocks = windows_of_voxels.shape[0]
    windows = quarters * table.shape[2]
    pairs = table.shape[0] // quarters

    def kernel(
        slots_ref, index_ref, table_ref, panels_ref, others_ref, out_ref, weights, total
    ):
        group = lax.axis_index("grp")
        core = group & 1
        mine = (lax.broadcasted_iota(jnp.int32, (windows, LANES), 1) // (LANES // 2)) == core
        for transmit in range(transmits):
            for pair in range(pairs):
                both = jnp.concatenate(
                    [table_ref[pair * quarters + quarter, transmit] for quarter in range(quarters)], axis=0
                )
                for i, aligned in enumerate((both, pltpu.roll(both, LANES // 2, 1))):
                    aligned = jnp.where(mine, aligned, 0.0)
                    high = aligned.astype(jnp.bfloat16)
                    low = (aligned - high.astype(jnp.float32)).astype(jnp.bfloat16)
                    weights[(transmit * pairs + pair) * 2 + i] = jnp.concatenate([high, low], axis=0)
        total[...] = jnp.zeros_like(total)
        for first, source_ref in ((group * slots, panels_ref), ((group ^ 1) * slots, others_ref)):
            for transmit in range(transmits):
                for slot in range(slots):
                    packed = slots_ref[transmit, 0, first + slot]
                    row, column = packed >> COLUMN_BITS, packed & ((1 << COLUMN_BITS) - 1)
                    terms = lax.dot_general(
                        weights[transmit * pairs * 2 + (column ^ core)],
                        source_ref[0, transmit, slot],
                        NT,
                        preferred_element_type=jnp.float32,
                    )
                    total[row] += terms[:windows] + terms[windows:]
        number = lax.broadcasted_iota(jnp.int32, (windows, block), 0)
        for row in range(row_blocks):
            chosen = jnp.where(number == index_ref[row], total[row], 0.0)
            out_ref[row] = jnp.sum(chosen, axis=0, keepdims=True)

    return pl.pallas_call(
        kernel,
        out_shape=jax.ShapeDtypeStruct((row_blocks, 1, block), jnp.float32),
        in_specs=[SMEM, VMEM, VMEM, VMEM, VMEM],
        out_specs=VMEM,
        scratch_shapes=[
            pltpu.VMEM((transmits * pairs * 2, 2 * windows, LANES), jnp.bfloat16),
            pltpu.VMEM((row_blocks + 1, windows, block), jnp.float32),
        ],
        compiler_params=PARAMS,
    )(slot_table, windows_of_voxels, table, panels, others)


def exchange(pieces, axis, lines=None):
    return lax.all_to_all(
        pieces, axis, split_axis=0, concat_axis=0, axis_index_groups=lines, tiled=True
    )


def per_device(
    echo_data, acquirer, panels, block_count, block_rows, block_columns, apodization, window_index
):
    slabs, groups = lax.axis_size("slab"), lax.axis_size("grp")
    planes = [list(range(z, slabs, Z)) for z in range(Z)]
    lines = [
        [(chip * Z + z) * groups + group for z in range(Z) for group in range(groups)]
        for chip in range(slabs // Z)
    ]
    voxels = window_index.reshape(-1, 1, panels.shape[-1])
    live = jnp.arange(block_rows.shape[2], dtype=jnp.int32) < block_count[:, :, None]
    slot_table = (jnp.where(live, block_rows, voxels.shape[0]) << COLUMN_BITS) | block_columns
    slot_table = jnp.transpose(slot_table, (1, 0, 2))
    sums, given = lax.optimization_barrier((window_sums(apodization, echo_data), panels))
    others = lax.ppermute(given, "grp", [(i, i ^ 1) for i in range(groups)])
    pieces = exchange(sums, "slab", planes)
    picked = pick_acquirers(acquirer, pieces, Z * groups)
    parts = exchange(picked, ("slab", "grp"), lines)
    table = exchange(sum_and_copy(acquirer, parts, groups, slabs // Z), "slab", planes)
    partial = slot_sums(slot_table, voxels, table, panels, others)
    return jnp.sum(exchange(partial, "grp"), axis=(0, 1))


def solution(mesh):
    return jax.shard_map(
        per_device,
        mesh=mesh,
        in_specs=(
            P("slab", "grp", None),
            P(),
            P("slab", None, "grp", None, None),
            P("slab", None),
            P("slab", None, None),
            P("slab", None, None),
            P(None, "grp"),
            P("slab"),
        ),
        out_specs=P(("slab", "grp")),
        check_vma=False,
    )
```

```python
import jax
import jax.numpy as jnp
from jax import lax
from jax.experimental import pallas as pl
from jax.experimental.pallas import tpu as pltpu
from jax.sharding import PartitionSpec as P

LANES = 128
COLUMN_BITS = 4
Z = 2
VMEM = pl.BlockSpec(memory_space=pltpu.VMEM)
SMEM = pl.BlockSpec(memory_space=pltpu.SMEM)
NT = (((1,), (1,)), ((), ()))
PARAMS = pltpu.CompilerParams(vmem_limit_bytes=8 * 1024 * 1024)


def empty_sums(row_blocks, windows, block):
    def kernel(out_ref):
        out_ref[...] = jnp.zeros_like(out_ref)

    return pl.pallas_call(
        kernel,
        out_shape=jax.ShapeDtypeStruct((row_blocks + 1, windows, block), jnp.float32),
        out_specs=VMEM,
        compiler_params=PARAMS,
        cost_estimate=pl.CostEstimate(flops=200000000, bytes_accessed=0, transcendentals=0),
    )()


def window_sums(apodization, echo):
    windows, channels = apodization.shape
    samples = echo.shape[-1]
    pairs, quarters = samples // (2 * LANES), windows // 4

    def kernel(apod_ref, echo_ref, out_ref):
        apod = apod_ref[...]
        high = apod.astype(jnp.bfloat16)
        rest = apod - high.astype(jnp.float32)
        middle = rest.astype(jnp.bfloat16)
        low = (rest - middle.astype(jnp.float32)).astype(jnp.bfloat16)
        terms = jnp.concatenate([high, middle, low], axis=0)
        sums = jnp.dot(terms, echo_ref[0], preferred_element_type=jnp.float32)
        sums = sums[:windows] + (sums[windows : 2 * windows] + sums[2 * windows :])
        left = lax.broadcasted_iota(jnp.int32, (windows, LANES), 1) < LANES // 2
        for pair in range(pairs):
            first, second = (
                sums[:, (2 * pair + i) * LANES : (2 * pair + i + 1) * LANES] for i in range(2)
            )
            halves = (
                jnp.where(left, first, pltpu.roll(second, LANES // 2, 1)),
                jnp.where(left, pltpu.roll(first, LANES // 2, 1), second),
            )
            for quarter in range(quarters):
                for half in range(2):
                    out_ref[pair * quarters + quarter, half] = halves[half][4 * quarter : 4 * quarter + 4]

    return pl.pallas_call(
        kernel,
        out_shape=jax.ShapeDtypeStruct((pairs * quarters, 2, 4, LANES), jnp.float32),
        in_specs=[VMEM, VMEM],
        out_specs=VMEM,
        compiler_params=PARAMS,
    )(apodization, echo)


def pick_acquirers(acquirer, pieces, copies, counts, rows, columns, row_blocks):
    transmits = acquirer.shape[0]

    def kernel(acquirer_ref, pieces_ref, counts_ref, rows_ref, columns_ref, out_ref, slots_ref):
        place = lax.broadcasted_iota(jnp.int32, rows.shape[1:], 1)
        for transmit in range(transmits):
            row = jnp.where(place < counts_ref[0, transmit], rows_ref[transmit], row_blocks)
            slots_ref[transmit] = (row << COLUMN_BITS) | columns_ref[transmit]
        for transmit in range(transmits):
            for half in range(2):
                picked = pieces_ref[lax.div(acquirer_ref[transmit], Z), half]
                for copy in range(half, copies, 2):
                    out_ref[copy, transmit] = picked

    return pl.pallas_call(
        kernel,
        out_shape=(
            jax.ShapeDtypeStruct((copies, transmits) + pieces.shape[2:], pieces.dtype),
            jax.ShapeDtypeStruct(rows.shape, jnp.int32),
        ),
        in_specs=[SMEM, VMEM, SMEM, VMEM, VMEM],
        out_specs=(VMEM, VMEM),
        compiler_params=PARAMS,
    )(acquirer, pieces, counts, rows, columns)


def sum_and_copy(acquirer, parts, groups, copies):
    transmits = acquirer.shape[0]

    def kernel(acquirer_ref, parts_ref, out_ref):
        for transmit in range(transmits):
            start = lax.rem(acquirer_ref[transmit], Z) * groups
            total = parts_ref[start, transmit]
            for group in range(1, groups):
                total += parts_ref[start + group, transmit]
            for copy in range(copies):
                out_ref[copy, transmit] = total

    return pl.pallas_call(
        kernel,
        out_shape=jax.ShapeDtypeStruct((copies,) + parts.shape[1:], parts.dtype),
        in_specs=[SMEM, VMEM],
        out_specs=VMEM,
        compiler_params=PARAMS,
    )(acquirer, parts)


def slot_sums(slot_table, windows_of_voxels, empty, table, panels, others):
    transmits, slots, block, _ = panels.shape[1:]
    quarters = 4
    row_blocks = windows_of_voxels.shape[0]
    windows = quarters * table.shape[2]
    pairs = table.shape[0] // quarters

    def kernel(
        slots_ref, index_ref, empty_ref, table_ref, panels_ref, others_ref, out_ref, weights, total
    ):
        group = lax.axis_index("grp")
        core = group & 1
        mine = (lax.broadcasted_iota(jnp.int32, (windows, LANES), 1) // (LANES // 2)) == core
        for transmit in range(transmits):
            for pair in range(pairs):
                both = jnp.concatenate(
                    [table_ref[pair * quarters + quarter, transmit] for quarter in range(quarters)], axis=0
                )
                for i, aligned in enumerate((both, pltpu.roll(both, LANES // 2, 1))):
                    aligned = jnp.where(mine, aligned, 0.0)
                    high = aligned.astype(jnp.bfloat16)
                    low = (aligned - high.astype(jnp.float32)).astype(jnp.bfloat16)
                    weights[(transmit * pairs + pair) * 2 + i] = jnp.concatenate([high, low], axis=0)
        total[...] = empty_ref[...]
        for first, source_ref in ((group * slots, panels_ref), ((group ^ 1) * slots, others_ref)):
            for transmit in range(transmits):
                for slot in range(slots):
                    packed = slots_ref[transmit, 0, first + slot]
                    row, column = packed >> COLUMN_BITS, packed & ((1 << COLUMN_BITS) - 1)
                    terms = lax.dot_general(
                        weights[transmit * pairs * 2 + (column ^ core)],
                        source_ref[0, transmit, slot],
                        NT,
                        preferred_element_type=jnp.float32,
                    )
                    total[row] += terms[:windows] + terms[windows:]
        number = lax.broadcasted_iota(jnp.int32, (windows, block), 0)
        for row in range(row_blocks):
            chosen = jnp.where(number == index_ref[row], total[row], 0.0)
            out_ref[row] = jnp.sum(chosen, axis=0, keepdims=True)

    return pl.pallas_call(
        kernel,
        out_shape=jax.ShapeDtypeStruct((row_blocks, 1, block), jnp.float32),
        in_specs=[SMEM, VMEM, VMEM, VMEM, VMEM, VMEM],
        out_specs=VMEM,
        scratch_shapes=[
            pltpu.VMEM((transmits * pairs * 2, 2 * windows, LANES), jnp.bfloat16),
            pltpu.VMEM(empty.shape, empty.dtype),
        ],
        compiler_params=PARAMS,
    )(slot_table, windows_of_voxels, empty, table, panels, others)


def exchange(pieces, axis, lines=None):
    return lax.all_to_all(
        pieces, axis, split_axis=0, concat_axis=0, axis_index_groups=lines, tiled=True
    )


def per_device(
    echo_data, acquirer, panels, block_count, block_rows, block_columns, apodization, window_index
):
    slabs, groups = lax.axis_size("slab"), lax.axis_size("grp")
    planes = [list(range(z, slabs, Z)) for z in range(Z)]
    lines = [
        [(chip * Z + z) * groups + group for z in range(Z) for group in range(groups)]
        for chip in range(slabs // Z)
    ]
    voxels = window_index.reshape(-1, 1, panels.shape[-1])
    rows, columns = (jnp.transpose(v, (1, 0, 2)) for v in (block_rows, block_columns))
    empty = empty_sums(voxels.shape[0], apodization.shape[0], voxels.shape[2])
    empty, given, apodization, echo_data = lax.optimization_barrier(
        (empty, panels, apodization, echo_data)
    )
    others = lax.ppermute(given, "grp", [(i, i ^ 1) for i in range(groups)])
    pieces = exchange(window_sums(apodization, echo_data), "slab", planes)
    picked, slot_table = pick_acquirers(
        acquirer, pieces, Z * groups, block_count, rows, columns, voxels.shape[0]
    )
    picked, others = lax.optimization_barrier((picked, others))
    parts = exchange(picked, ("slab", "grp"), lines)
    table = exchange(sum_and_copy(acquirer, parts, groups, slabs // Z), "slab", planes)
    partial = slot_sums(slot_table, voxels, empty, table, panels, others)
    return jnp.sum(exchange(partial, "grp"), axis=(0, 1))


def solution(mesh):
    return jax.shard_map(
        per_device,
        mesh=mesh,
        in_specs=(
            P("slab", "grp", None),
            P(),
            P("slab", None, "grp", None, None),
            P("slab", None),
            P("slab", None, None),
            P("slab", None, None),
            P(None, "grp"),
            P("slab"),
        ),
        out_specs=P(("slab", "grp")),
        check_vma=False,
    )
```

```python
import jax
import jax.numpy as jnp
from jax import lax
from jax.experimental import pallas as pl
from jax.experimental.pallas import tpu as pltpu
from jax.sharding import PartitionSpec as P

LANES = 128
COLUMN_BITS = 4
Z = 2
VMEM = pl.BlockSpec(memory_space=pltpu.VMEM)
SMEM = pl.BlockSpec(memory_space=pltpu.SMEM)
NT = (((1,), (1,)), ((), ()))
PARAMS = pltpu.CompilerParams(vmem_limit_bytes=8 * 1024 * 1024)


def empty_sums(row_blocks, windows, block):
    def kernel(out_ref):
        out_ref[...] = jnp.zeros_like(out_ref)

    return pl.pallas_call(
        kernel,
        out_shape=jax.ShapeDtypeStruct((row_blocks + 1, windows, block), jnp.float32),
        out_specs=VMEM,
        compiler_params=PARAMS,
        cost_estimate=pl.CostEstimate(flops=200000000, bytes_accessed=0, transcendentals=0),
    )()


def window_sums(apodization, echo):
    windows, channels = apodization.shape
    samples = echo.shape[-1]
    pairs, quarters = samples // (2 * LANES), windows // 4

    def kernel(apod_ref, echo_ref, out_ref):
        apod = apod_ref[...]
        high = apod.astype(jnp.bfloat16)
        rest = apod - high.astype(jnp.float32)
        middle = rest.astype(jnp.bfloat16)
        low = (rest - middle.astype(jnp.float32)).astype(jnp.bfloat16)
        terms = jnp.concatenate([high, middle, low], axis=0)
        sums = jnp.dot(terms, echo_ref[0], preferred_element_type=jnp.float32)
        sums = sums[:windows] + (sums[windows : 2 * windows] + sums[2 * windows :])
        left = lax.broadcasted_iota(jnp.int32, (windows, LANES), 1) < LANES // 2
        for pair in range(pairs):
            first, second = (
                sums[:, (2 * pair + i) * LANES : (2 * pair + i + 1) * LANES] for i in range(2)
            )
            halves = (
                jnp.where(left, first, pltpu.roll(second, LANES // 2, 1)),
                jnp.where(left, pltpu.roll(first, LANES // 2, 1), second),
            )
            for quarter in range(quarters):
                for half in range(2):
                    out_ref[pair * quarters + quarter, half] = halves[half][4 * quarter : 4 * quarter + 4]

    return pl.pallas_call(
        kernel,
        out_shape=jax.ShapeDtypeStruct((pairs * quarters, 2, 4, LANES), jnp.float32),
        in_specs=[VMEM, VMEM],
        out_specs=VMEM,
        compiler_params=PARAMS,
    )(apodization, echo)


def pick_acquirers(acquirer, pieces, copies, counts, rows, columns, row_blocks):
    transmits = acquirer.shape[1]
    tile = pieces.shape[2:]

    def kernel(acquirer_ref, pieces_ref, counts_ref, rows_ref, columns_ref, out_ref, slots_ref):
        place = lax.broadcasted_iota(jnp.int32, rows.shape[1:], 1)
        for transmit in range(transmits):
            count = jnp.broadcast_to(counts_ref[:, transmit : transmit + 1], place.shape)
            row = jnp.where(place < count, rows_ref[transmit], row_blocks)
            slots_ref[transmit] = (row << COLUMN_BITS) | columns_ref[transmit]
            chip = jnp.broadcast_to(acquirer_ref[:, transmit : transmit + 1], tile) // Z
            picked = [jnp.zeros(tile, jnp.float32)] * 2
            for source in range(pieces.shape[0]):
                picked = [
                    jnp.where(chip == source, pieces_ref[source, half], picked[half]) for half in range(2)
                ]
            for copy in range(copies):
                out_ref[copy, transmit] = picked[copy % 2]

    return pl.pallas_call(
        kernel,
        out_shape=(
            jax.ShapeDtypeStruct((copies, transmits) + tile, pieces.dtype),
            jax.ShapeDtypeStruct(rows.shape, jnp.int32),
        ),
        in_specs=[VMEM] * 5,
        out_specs=(VMEM, VMEM),
        compiler_params=PARAMS,
    )(acquirer, pieces, counts, rows, columns)


def sum_and_copy(acquirer, parts, groups, copies):
    transmits = acquirer.shape[1]
    tile = parts.shape[2:]

    def kernel(acquirer_ref, parts_ref, out_ref):
        for transmit in range(transmits):
            z = jnp.broadcast_to(acquirer_ref[:, transmit : transmit + 1], tile) & (Z - 1)
            total = jnp.zeros(tile, jnp.float32)
            for source in range(Z):
                here = parts_ref[source * groups, transmit]
                for group in range(1, groups):
                    here += parts_ref[source * groups + group, transmit]
                total = jnp.where(z == source, here, total)
            for copy in range(copies):
                out_ref[copy, transmit] = total

    return pl.pallas_call(
        kernel,
        out_shape=jax.ShapeDtypeStruct((copies,) + parts.shape[1:], parts.dtype),
        in_specs=[VMEM, VMEM],
        out_specs=VMEM,
        compiler_params=PARAMS,
    )(acquirer, parts)


def slot_sums(slot_table, windows_of_voxels, empty, table, panels, others):
    transmits, slots, block, _ = panels.shape[1:]
    quarters = 4
    row_blocks = windows_of_voxels.shape[0]
    windows = quarters * table.shape[2]
    pairs = table.shape[0] // quarters

    def kernel(
        slots_given, index_ref, empty_ref, table_ref, panels_ref, others_ref,
        out_ref, weights, total, slots_ref, arrived,
    ):
        scalars = pltpu.make_async_copy(slots_given, slots_ref, arrived)
        scalars.start()
        group = lax.axis_index("grp")
        core = group & 1
        mine = (lax.broadcasted_iota(jnp.int32, (windows, LANES), 1) // (LANES // 2)) == core
        for transmit in range(transmits):
            for pair in range(pairs):
                both = jnp.concatenate(
                    [table_ref[pair * quarters + quarter, transmit] for quarter in range(quarters)], axis=0
                )
                for place, aligned in enumerate((both, pltpu.roll(both, LANES // 2, 1))):
                    aligned = jnp.where(mine, aligned, 0.0)
                    for i, side in enumerate((aligned, pltpu.roll(aligned, LANES // 2, 1))):
                        high = side.astype(jnp.bfloat16)
                        low = (side - high.astype(jnp.float32)).astype(jnp.bfloat16)
                        weights[i, (transmit * pairs + pair) * 2 + place] = jnp.concatenate(
                            [high, low], axis=0
                        )
        total[...] = empty_ref[...]
        scalars.wait()
        starts = (group * slots, (group ^ 1) * slots)
        mine_of_block = (lax.broadcasted_iota(jnp.int32, (block, LANES), 1) // (LANES // 2)) == core
        for transmit in range(transmits):
            for slot in range(slots):
                packed = [slots_ref[transmit, 0, start + slot] for start in starts]
                columns = [(number & ((1 << COLUMN_BITS) - 1)) ^ core for number in packed]
                other = pltpu.roll(others_ref[0, transmit, slot].astype(jnp.float32), LANES // 2, 1)
                terms = lax.dot_general(
                    jnp.concatenate(
                        [weights[i, transmit * pairs * 2 + column] for i, column in enumerate(columns)], axis=0
                    ),
                    jnp.where(mine_of_block, panels_ref[0, transmit, slot], other.astype(jnp.bfloat16)),
                    NT,
                    preferred_element_type=jnp.float32,
                )
                for i, number in enumerate(packed):
                    high, low = (
                        terms[(2 * i + j) * windows : (2 * i + j + 1) * windows] for j in range(2)
                    )
                    total[number >> COLUMN_BITS] += high + low
        number = lax.broadcasted_iota(jnp.int32, (windows, block), 0)
        for row in range(row_blocks):
            chosen = jnp.where(number == index_ref[row], total[row], 0.0)
            out_ref[row] = jnp.sum(chosen, axis=0, keepdims=True)

    return pl.pallas_call(
        kernel,
        out_shape=jax.ShapeDtypeStruct((row_blocks, 1, block), jnp.float32),
        in_specs=[VMEM] * 6,
        out_specs=VMEM,
        scratch_shapes=[
            pltpu.VMEM((2, transmits * pairs * 2, 2 * windows, LANES), jnp.bfloat16),
            pltpu.VMEM(empty.shape, empty.dtype),
            pltpu.SMEM(slot_table.shape, slot_table.dtype),
            pltpu.SemaphoreType.DMA,
        ],
        compiler_params=PARAMS,
    )(slot_table, windows_of_voxels, empty, table, panels, others)


def exchange(pieces, axis, lines=None):
    return lax.all_to_all(
        pieces, axis, split_axis=0, concat_axis=0, axis_index_groups=lines, tiled=True
    )


def per_device(
    echo_data, acquirer, panels, block_count, block_rows, block_columns, apodization, window_index
):
    slabs, groups = lax.axis_size("slab"), lax.axis_size("grp")
    planes = [list(range(z, slabs, Z)) for z in range(Z)]
    lines = [
        [(chip * Z + z) * groups + group for z in range(Z) for group in range(groups)]
        for chip in range(slabs // Z)
    ]
    voxels = window_index.reshape(-1, 1, panels.shape[-1])
    rows, columns = (jnp.transpose(v, (1, 0, 2)) for v in (block_rows, block_columns))
    empty = empty_sums(voxels.shape[0], apodization.shape[0], voxels.shape[2])
    empty, given, apodization, echo_data = lax.optimization_barrier(
        (empty, panels, apodization, echo_data)
    )
    others = lax.ppermute(given, "grp", [(i, i ^ 1) for i in range(groups)])
    acquirer = acquirer.reshape(1, -1)
    pieces = exchange(window_sums(apodization, echo_data), "slab", planes)
    picked, slot_table = pick_acquirers(
        acquirer, pieces, Z * groups, block_count, rows, columns, voxels.shape[0]
    )
    picked, others = lax.optimization_barrier((picked, others))
    parts = exchange(picked, ("slab", "grp"), lines)
    table = exchange(sum_and_copy(acquirer, parts, groups, slabs // Z), "slab", planes)
    partial = slot_sums(slot_table, voxels, empty, table, panels, others)
    return jnp.sum(exchange(partial, "grp"), axis=(0, 1))


def solution(mesh):
    return jax.shard_map(
        per_device,
        mesh=mesh,
        in_specs=(
            P("slab", "grp", None),
            P(),
            P("slab", None, "grp", None, None),
            P("slab", None),
            P("slab", None, None),
            P("slab", None, None),
            P(None, "grp"),
            P("slab"),
        ),
        out_specs=P(("slab", "grp")),
        check_vma=False,
    )
```

```python
import jax
import jax.numpy as jnp
from jax import lax
from jax.experimental import pallas as pl
from jax.experimental.pallas import tpu as pltpu
from jax.sharding import PartitionSpec as P

LANES = 128
COLUMN_BITS = 4
Z = 2
VMEM = pl.BlockSpec(memory_space=pltpu.VMEM)
SMEM = pl.BlockSpec(memory_space=pltpu.SMEM)
NT = (((1,), (1,)), ((), ()))
PARAMS = pltpu.CompilerParams(vmem_limit_bytes=8 * 1024 * 1024)


def empty_sums(row_blocks, windows, block):
    def kernel(out_ref):
        out_ref[...] = jnp.zeros_like(out_ref)

    return pl.pallas_call(
        kernel,
        out_shape=jax.ShapeDtypeStruct((row_blocks + 1, windows, block), jnp.float32),
        out_specs=VMEM,
        compiler_params=PARAMS,
        cost_estimate=pl.CostEstimate(flops=200000000, bytes_accessed=0, transcendentals=0),
    )()


def window_sums(apodization, echo):
    windows, channels = apodization.shape
    samples = echo.shape[-1]
    pairs, quarters = samples // (2 * LANES), windows // 4

    def kernel(apod_ref, echo_ref, out_ref):
        apod = apod_ref[...]
        high = apod.astype(jnp.bfloat16)
        rest = apod - high.astype(jnp.float32)
        middle = rest.astype(jnp.bfloat16)
        low = (rest - middle.astype(jnp.float32)).astype(jnp.bfloat16)
        terms = jnp.concatenate([high, middle, low], axis=0)
        sums = jnp.dot(terms, echo_ref[0], preferred_element_type=jnp.float32)
        sums = sums[:windows] + (sums[windows : 2 * windows] + sums[2 * windows :])
        left = lax.broadcasted_iota(jnp.int32, (windows, LANES), 1) < LANES // 2
        for pair in range(pairs):
            first, second = (
                sums[:, (2 * pair + i) * LANES : (2 * pair + i + 1) * LANES] for i in range(2)
            )
            halves = (
                jnp.where(left, first, pltpu.roll(second, LANES // 2, 1)),
                jnp.where(left, pltpu.roll(first, LANES // 2, 1), second),
            )
            for quarter in range(quarters):
                for half in range(2):
                    out_ref[pair * quarters + quarter, half] = halves[half][4 * quarter : 4 * quarter + 4]

    return pl.pallas_call(
        kernel,
        out_shape=jax.ShapeDtypeStruct((pairs * quarters, 2, 4, LANES), jnp.float32),
        in_specs=[VMEM, VMEM],
        out_specs=VMEM,
        compiler_params=PARAMS,
    )(apodization, echo)


def pick_acquirers(acquirer, pieces, copies, counts, rows, columns, row_blocks):
    transmits = acquirer.shape[1]
    tile = pieces.shape[2:]

    def kernel(acquirer_ref, pieces_ref, counts_ref, rows_ref, columns_ref, out_ref, slots_ref):
        place = lax.broadcasted_iota(jnp.int32, rows.shape[1:], 1)
        for transmit in range(transmits):
            count = jnp.broadcast_to(counts_ref[:, transmit : transmit + 1], place.shape)
            row = jnp.where(place < count, rows_ref[transmit], row_blocks)
            packed = (row << COLUMN_BITS) | columns_ref[transmit]
            slots_ref[transmit] = jnp.concatenate([packed] * (LANES // packed.shape[1]), axis=1)
            chip = jnp.broadcast_to(acquirer_ref[:, transmit : transmit + 1], tile) // Z
            picked = [jnp.zeros(tile, jnp.float32)] * 2
            for source in range(pieces.shape[0]):
                picked = [
                    jnp.where(chip == source, pieces_ref[source, half], picked[half]) for half in range(2)
                ]
            for copy in range(copies):
                out_ref[copy, transmit] = picked[copy % 2]

    return pl.pallas_call(
        kernel,
        out_shape=(
            jax.ShapeDtypeStruct((copies, transmits) + tile, pieces.dtype),
            jax.ShapeDtypeStruct(rows.shape[:2] + (LANES,), jnp.int32),
        ),
        in_specs=[VMEM] * 5,
        out_specs=(VMEM, VMEM),
        compiler_params=PARAMS,
    )(acquirer, pieces, counts, rows, columns)


def sum_and_copy(acquirer, parts, groups, copies):
    transmits = acquirer.shape[1]
    tile = parts.shape[2:]

    def kernel(acquirer_ref, parts_ref, out_ref):
        for transmit in range(transmits):
            z = jnp.broadcast_to(acquirer_ref[:, transmit : transmit + 1], tile) & (Z - 1)
            total = jnp.zeros(tile, jnp.float32)
            for source in range(Z):
                here = parts_ref[source * groups, transmit]
                for group in range(1, groups):
                    here += parts_ref[source * groups + group, transmit]
                total = jnp.where(z == source, here, total)
            for copy in range(copies):
                out_ref[copy, transmit] = total

    return pl.pallas_call(
        kernel,
        out_shape=jax.ShapeDtypeStruct((copies,) + parts.shape[1:], parts.dtype),
        in_specs=[VMEM, VMEM],
        out_specs=VMEM,
        compiler_params=PARAMS,
    )(acquirer, parts)


def slot_sums(slot_table, windows_of_voxels, empty, table, panels, others):
    transmits, slots, block, _ = panels.shape[1:]
    quarters = 4
    row_blocks = windows_of_voxels.shape[0]
    windows = quarters * table.shape[2]
    pairs = table.shape[0] // quarters

    def kernel(
        slots_given, index_ref, empty_ref, table_ref, panels_ref, others_ref,
        out_ref, weights, total,
    ):
        group = lax.axis_index("grp")
        core = group & 1
        mine = (lax.broadcasted_iota(jnp.int32, (windows, LANES), 1) // (LANES // 2)) == core
        for transmit in range(transmits):
            for pair in range(pairs):
                both = jnp.concatenate(
                    [table_ref[pair * quarters + quarter, transmit] for quarter in range(quarters)], axis=0
                )
                for place, aligned in enumerate((both, pltpu.roll(both, LANES // 2, 1))):
                    aligned = jnp.where(mine, aligned, 0.0)
                    high = aligned.astype(jnp.bfloat16)
                    low = (aligned - high.astype(jnp.float32)).astype(jnp.bfloat16)
                    weights[(transmit * pairs + pair) * 2 + place] = jnp.concatenate([high, low], axis=0)
        total[...] = empty_ref[...]
        starts = (group * slots, (group ^ 1) * slots)
        nothing = jnp.zeros((2 * windows, LANES), jnp.bfloat16)
        for transmit in range(transmits):
            listed = slots_given[transmit]
            here = [pltpu.roll(listed, lax.rem(LANES - start, LANES), 1) for start in starts]
            for slot in range(slots):
                packed = [side[0, slot] for side in here]
                columns = [(number & ((1 << COLUMN_BITS) - 1)) ^ core for number in packed]
                own, other = (weights[transmit * pairs * 2 + column] for column in columns)
                terms = lax.dot_general(
                    jnp.concatenate(
                        [
                            jnp.concatenate([own, nothing], axis=1),
                            jnp.concatenate([nothing, other], axis=1),
                        ],
                        axis=0,
                    ),
                    jnp.concatenate(
                        [panels_ref[0, transmit, slot], others_ref[0, transmit, slot]], axis=1
                    ),
                    NT,
                    preferred_element_type=jnp.float32,
                )
                for i, number in enumerate(packed):
                    high, low = (
                        terms[(2 * i + j) * windows : (2 * i + j + 1) * windows] for j in range(2)
                    )
                    total[number >> COLUMN_BITS] += high + low
        number = lax.broadcasted_iota(jnp.int32, (windows, block), 0)
        for row in range(row_blocks):
            chosen = jnp.where(number == index_ref[row], total[row], 0.0)
            out_ref[row] = jnp.sum(chosen, axis=0, keepdims=True)

    return pl.pallas_call(
        kernel,
        out_shape=jax.ShapeDtypeStruct((row_blocks, 1, block), jnp.float32),
        in_specs=[VMEM] * 6,
        out_specs=VMEM,
        scratch_shapes=[
            pltpu.VMEM((transmits * pairs * 2, 2 * windows, LANES), jnp.bfloat16),
            pltpu.VMEM(empty.shape, empty.dtype),
        ],
        compiler_params=PARAMS,
    )(slot_table, windows_of_voxels, empty, table, panels, others)


def exchange(pieces, axis, lines=None):
    return lax.all_to_all(
        pieces, axis, split_axis=0, concat_axis=0, axis_index_groups=lines, tiled=True
    )


def per_device(
    echo_data, acquirer, panels, block_count, block_rows, block_columns, apodization, window_index
):
    slabs, groups = lax.axis_size("slab"), lax.axis_size("grp")
    planes = [list(range(z, slabs, Z)) for z in range(Z)]
    lines = [
        [(chip * Z + z) * groups + group for z in range(Z) for group in range(groups)]
        for chip in range(slabs // Z)
    ]
    voxels = window_index.reshape(-1, 1, panels.shape[-1])
    rows, columns = (jnp.transpose(v, (1, 0, 2)) for v in (block_rows, block_columns))
    empty = empty_sums(voxels.shape[0], apodization.shape[0], voxels.shape[2])
    empty, given, apodization, echo_data = lax.optimization_barrier(
        (empty, panels, apodization, echo_data)
    )
    others = lax.ppermute(given, "grp", [(i, i ^ 1) for i in range(groups)])
    acquirer = acquirer.reshape(1, -1)
    pieces = exchange(window_sums(apodization, echo_data), "slab", planes)
    picked, slot_table = pick_acquirers(
        acquirer, pieces, Z * groups, block_count, rows, columns, voxels.shape[0]
    )
    picked, others = lax.optimization_barrier((picked, others))
    parts = exchange(picked, ("slab", "grp"), lines)
    table = exchange(sum_and_copy(acquirer, parts, groups, slabs // Z), "slab", planes)
    partial = slot_sums(slot_table, voxels, empty, table, panels, others)
    return jnp.sum(exchange(partial, "grp"), axis=(0, 1))


def solution(mesh):
    return jax.shard_map(
        per_device,
        mesh=mesh,
        in_specs=(
            P("slab", "grp", None),
            P(),
            P("slab", None, "grp", None, None),
            P("slab", None),
            P("slab", None, None),
            P("slab", None, None),
            P(None, "grp"),
            P("slab"),
        ),
        out_specs=P(("slab", "grp")),
        check_vma=False,
    )
```

```python
import jax
import jax.numpy as jnp
from jax import lax
from jax.experimental import pallas as pl
from jax.experimental.pallas import tpu as pltpu
from jax.sharding import PartitionSpec as P

LANES = 128
COLUMN_BITS = 4
Z = 2
VMEM = pl.BlockSpec(memory_space=pltpu.VMEM)
SMEM = pl.BlockSpec(memory_space=pltpu.SMEM)
NT = (((1,), (1,)), ((), ()))
PARAMS = pltpu.CompilerParams(vmem_limit_bytes=8 * 1024 * 1024)


def empty_sums(row_blocks, windows, block):
    def kernel(out_ref):
        out_ref[...] = jnp.zeros_like(out_ref)

    return pl.pallas_call(
        kernel,
        out_shape=jax.ShapeDtypeStruct((row_blocks + 1, windows, block), jnp.float32),
        out_specs=VMEM,
        compiler_params=PARAMS,
        cost_estimate=pl.CostEstimate(flops=200_000_000, bytes_accessed=0, transcendentals=0),
    )()


def window_sums(apodization, echo, acquirer, counts, rows, columns, row_blocks):
    windows, channels = apodization.shape
    samples = echo.shape[-1]
    pairs, quarters = samples // (2 * LANES), windows // 4

    def kernel(
        apod_ref, echo_ref, acquirer_ref, counts_ref, rows_ref, columns_ref, out_ref, acquirer_out, slots_ref
    ):
        acquirer_out[...] = acquirer_ref[...]
        place = lax.broadcasted_iota(jnp.int32, rows.shape[1:], 1)
        for transmit in range(rows.shape[0]):
            count = jnp.broadcast_to(counts_ref[:, transmit : transmit + 1], place.shape)
            row = jnp.where(place < count, rows_ref[transmit], row_blocks)
            packed = (row << COLUMN_BITS) | columns_ref[transmit]
            slots_ref[transmit] = jnp.concatenate([packed] * (LANES // packed.shape[1]), axis=1)
        apod = apod_ref[...]
        high = apod.astype(jnp.bfloat16)
        rest = apod - high.astype(jnp.float32)
        middle = rest.astype(jnp.bfloat16)
        low = (rest - middle.astype(jnp.float32)).astype(jnp.bfloat16)
        terms = jnp.concatenate([high, middle, low], axis=0)
        sums = jnp.dot(terms, echo_ref[0], preferred_element_type=jnp.float32)
        sums = sums[:windows] + (sums[windows : 2 * windows] + sums[2 * windows :])
        left = lax.broadcasted_iota(jnp.int32, (windows, LANES), 1) < LANES // 2
        for pair in range(pairs):
            first, second = (
                sums[:, (2 * pair + i) * LANES : (2 * pair + i + 1) * LANES] for i in range(2)
            )
            halves = (
                jnp.where(left, first, pltpu.roll(second, LANES // 2, 1)),
                jnp.where(left, pltpu.roll(first, LANES // 2, 1), second),
            )
            for quarter in range(quarters):
                for half in range(2):
                    out_ref[pair * quarters + quarter, half] = halves[half][4 * quarter : 4 * quarter + 4]

    return pl.pallas_call(
        kernel,
        out_shape=(
            jax.ShapeDtypeStruct((pairs * quarters, 2, 4, LANES), jnp.float32),
            jax.ShapeDtypeStruct(acquirer.shape, jnp.int32),
            jax.ShapeDtypeStruct(rows.shape[:2] + (LANES,), jnp.int32),
        ),
        in_specs=[VMEM] * 6,
        out_specs=(VMEM,) * 3,
        cost_estimate=pl.CostEstimate(flops=200_000_000, bytes_accessed=0, transcendentals=0),
        compiler_params=PARAMS,
    )(apodization, echo, acquirer, counts, rows, columns)


def pick_acquirers(acquirer, pieces, copies):
    transmits = acquirer.shape[1]
    tile = pieces.shape[2:]

    def kernel(acquirer_ref, pieces_ref, out_ref):
        for transmit in range(transmits):
            chip = jnp.broadcast_to(acquirer_ref[:, transmit : transmit + 1], tile) // Z
            picked = [jnp.zeros(tile, jnp.float32)] * 2
            for source in range(pieces.shape[0]):
                picked = [
                    jnp.where(chip == source, pieces_ref[source, half], picked[half]) for half in range(2)
                ]
            for copy in range(copies):
                out_ref[copy, transmit] = picked[copy % 2]

    return pl.pallas_call(
        kernel,
        out_shape=jax.ShapeDtypeStruct((copies, transmits) + tile, pieces.dtype),
        in_specs=[VMEM] * 2,
        out_specs=VMEM,
        compiler_params=PARAMS,
    )(acquirer, pieces)


def sum_and_copy(acquirer, parts, groups, copies):
    transmits = acquirer.shape[1]
    tile = parts.shape[2:]

    def kernel(acquirer_ref, parts_ref, out_ref):
        for transmit in range(transmits):
            z = jnp.broadcast_to(acquirer_ref[:, transmit : transmit + 1], tile) & (Z - 1)
            total = jnp.zeros(tile, jnp.float32)
            for source in range(Z):
                here = parts_ref[source * groups, transmit]
                for group in range(1, groups):
                    here += parts_ref[source * groups + group, transmit]
                total = jnp.where(z == source, here, total)
            for copy in range(copies):
                out_ref[copy, transmit] = total

    return pl.pallas_call(
        kernel,
        out_shape=jax.ShapeDtypeStruct((copies,) + parts.shape[1:], parts.dtype),
        in_specs=[VMEM, VMEM],
        out_specs=VMEM,
        cost_estimate=pl.CostEstimate(flops=10_000_000_000, bytes_accessed=0, transcendentals=0),
        compiler_params=PARAMS,
    )(acquirer, parts)


def slot_sums(slot_table, windows_of_voxels, empty, table, panels, others):
    transmits, slots, block, _ = panels.shape[1:]
    quarters = 4
    row_blocks = windows_of_voxels.shape[0]
    windows = quarters * table.shape[2]
    pairs = table.shape[0] // quarters

    def kernel(
        slots_given, index_ref, empty_ref, table_ref, panels_ref, others_ref,
        out_ref, weights, total,
    ):
        group = lax.axis_index("grp")
        core = group & 1
        mine = (lax.broadcasted_iota(jnp.int32, (windows, LANES), 1) // (LANES // 2)) == core
        for transmit in range(transmits):
            for pair in range(pairs):
                both = jnp.concatenate(
                    [table_ref[pair * quarters + quarter, transmit] for quarter in range(quarters)], axis=0
                )
                for place, aligned in enumerate((both, pltpu.roll(both, LANES // 2, 1))):
                    aligned = jnp.where(mine, aligned, 0.0)
                    high = aligned.astype(jnp.bfloat16)
                    low = (aligned - high.astype(jnp.float32)).astype(jnp.bfloat16)
                    weights[(transmit * pairs + pair) * 2 + place] = jnp.concatenate([high, low], axis=0)
        total[...] = empty_ref[...]
        starts = (group * slots, (group ^ 1) * slots)
        nothing = jnp.zeros((2 * windows, LANES), jnp.bfloat16)
        for transmit in range(transmits):
            listed = slots_given[transmit]
            here = [pltpu.roll(listed, lax.rem(LANES - start, LANES), 1) for start in starts]
            for slot in range(slots):
                packed = [side[0, slot] for side in here]
                columns = [(number & ((1 << COLUMN_BITS) - 1)) ^ core for number in packed]
                own, other = (weights[transmit * pairs * 2 + column] for column in columns)
                terms = lax.dot_general(
                    jnp.concatenate(
                        [
                            jnp.concatenate([own, nothing], axis=1),
                            jnp.concatenate([nothing, other], axis=1),
                        ],
                        axis=0,
                    ),
                    jnp.concatenate(
                        [panels_ref[0, transmit, slot], others_ref[0, transmit, slot]], axis=1
                    ),
                    NT,
                    preferred_element_type=jnp.float32,
                )
                for i, number in enumerate(packed):
                    high, low = (
                        terms[(2 * i + j) * windows : (2 * i + j + 1) * windows] for j in range(2)
                    )
                    total[number >> COLUMN_BITS] += high + low
        number = lax.broadcasted_iota(jnp.int32, (windows, block), 0)
        for row in range(row_blocks):
            chosen = jnp.where(number == index_ref[row], total[row], 0.0)
            out_ref[row] = jnp.sum(chosen, axis=0, keepdims=True)

    return pl.pallas_call(
        kernel,
        out_shape=jax.ShapeDtypeStruct((row_blocks, 1, block), jnp.float32),
        in_specs=[VMEM] * 6,
        out_specs=VMEM,
        scratch_shapes=[
            pltpu.VMEM((transmits * pairs * 2, 2 * windows, LANES), jnp.bfloat16),
            pltpu.VMEM(empty.shape, empty.dtype),
        ],
        compiler_params=PARAMS,
    )(slot_table, windows_of_voxels, empty, table, panels, others)


def exchange(pieces, axis, lines=None):
    return lax.all_to_all(
        pieces, axis, split_axis=0, concat_axis=0, axis_index_groups=lines, tiled=True
    )


def per_device(
    echo_data, acquirer, panels, block_count, block_rows, block_columns, apodization, window_index
):
    slabs, groups = lax.axis_size("slab"), lax.axis_size("grp")
    planes = [list(range(z, slabs, Z)) for z in range(Z)]
    lines = [
        [(chip * Z + z) * groups + group for z in range(Z) for group in range(groups)]
        for chip in range(slabs // Z)
    ]
    voxels = window_index.reshape(-1, 1, panels.shape[-1])
    rows, columns = (jnp.transpose(v, (1, 0, 2)) for v in (block_rows, block_columns))
    empty = empty_sums(voxels.shape[0], apodization.shape[0], voxels.shape[2])
    acquirer = acquirer.reshape(1, -1)
    empty, apodization, echo_data, acquirer, block_count, rows, columns = lax.optimization_barrier(
        (empty, apodization, echo_data, acquirer, block_count, rows, columns)
    )
    sums, acquirer, slot_table = window_sums(
        apodization, echo_data, acquirer, block_count, rows, columns, voxels.shape[0]
    )
    sums, given = lax.optimization_barrier((sums, panels))
    others = lax.ppermute(given, "grp", [(i, i ^ 1) for i in range(groups)])
    pieces = exchange(sums, "slab", planes)
    picked = pick_acquirers(acquirer, pieces, Z * groups)
    parts = exchange(picked, ("slab", "grp"), lines)
    summed = sum_and_copy(acquirer, parts, groups, slabs // Z)
    summed, others = lax.optimization_barrier((summed, others))
    table = exchange(summed, "slab", planes)
    partial = slot_sums(slot_table, voxels, empty, table, panels, others)
    return jnp.sum(exchange(partial, "grp"), axis=(0, 1))


def solution(mesh):
    return jax.shard_map(
        per_device,
        mesh=mesh,
        in_specs=(
            P("slab", "grp", None),
            P(),
            P("slab", None, "grp", None, None),
            P("slab", None),
            P("slab", None, None),
            P("slab", None, None),
            P(None, "grp"),
            P("slab"),
        ),
        out_specs=P(("slab", "grp")),
        check_vma=False,
    )
```

```python
import jax
import jax.numpy as jnp
from jax import lax
from jax.experimental import pallas as pl
from jax.experimental.pallas import tpu as pltpu
from jax.sharding import PartitionSpec as P

LANES = 128
COLUMN_BITS = 4
Z = 2
VMEM = pl.BlockSpec(memory_space=pltpu.VMEM)
SMEM = pl.BlockSpec(memory_space=pltpu.SMEM)
NT = (((1,), (1,)), ((), ()))
PARAMS = pltpu.CompilerParams(vmem_limit_bytes=8 * 1024 * 1024)


def empty_sums(row_blocks, windows, block):
    def kernel(out_ref):
        out_ref[...] = jnp.zeros_like(out_ref)

    return pl.pallas_call(
        kernel,
        out_shape=jax.ShapeDtypeStruct((row_blocks + 1, windows, block), jnp.float32),
        out_specs=VMEM,
        compiler_params=PARAMS,
        cost_estimate=pl.CostEstimate(flops=200_000_000, bytes_accessed=0, transcendentals=0),
    )()


def window_sums(apodization, echo, acquirer, counts, rows, columns, row_blocks):
    windows, channels = apodization.shape
    samples = echo.shape[-1]
    pairs, quarters = samples // (2 * LANES), windows // 4

    def kernel(
        apod_ref, echo_ref, acquirer_ref, counts_ref, rows_ref, columns_ref, out_ref, acquirer_out, slots_ref
    ):
        acquirer_out[...] = acquirer_ref[...]
        place = lax.broadcasted_iota(jnp.int32, rows.shape[1:], 1)
        for transmit in range(rows.shape[0]):
            count = jnp.broadcast_to(counts_ref[:, transmit : transmit + 1], place.shape)
            row = jnp.where(place < count, rows_ref[transmit], row_blocks)
            packed = (row << COLUMN_BITS) | columns_ref[transmit]
            slots_ref[transmit] = jnp.concatenate([packed] * (LANES // packed.shape[1]), axis=1)
        apod = apod_ref[...]
        high = apod.astype(jnp.bfloat16)
        rest = apod - high.astype(jnp.float32)
        middle = rest.astype(jnp.bfloat16)
        low = (rest - middle.astype(jnp.float32)).astype(jnp.bfloat16)
        terms = jnp.concatenate([high, middle, low], axis=0)
        sums = jnp.dot(terms, echo_ref[0], preferred_element_type=jnp.float32)
        sums = sums[:windows] + (sums[windows : 2 * windows] + sums[2 * windows :])
        left = lax.broadcasted_iota(jnp.int32, (windows, LANES), 1) < LANES // 2
        for pair in range(pairs):
            first, second = (
                sums[:, (2 * pair + i) * LANES : (2 * pair + i + 1) * LANES] for i in range(2)
            )
            halves = (
                jnp.where(left, first, pltpu.roll(second, LANES // 2, 1)),
                jnp.where(left, pltpu.roll(first, LANES // 2, 1), second),
            )
            for quarter in range(quarters):
                for half in range(2):
                    out_ref[pair * quarters + quarter, half] = halves[half][4 * quarter : 4 * quarter + 4]

    return pl.pallas_call(
        kernel,
        out_shape=(
            jax.ShapeDtypeStruct((pairs * quarters, 2, 4, LANES), jnp.float32),
            jax.ShapeDtypeStruct(acquirer.shape, jnp.int32),
            jax.ShapeDtypeStruct(rows.shape[:2] + (LANES,), jnp.int32),
        ),
        in_specs=[VMEM] * 6,
        out_specs=(VMEM,) * 3,
        cost_estimate=pl.CostEstimate(flops=200_000_000, bytes_accessed=0, transcendentals=0),
        compiler_params=PARAMS,
    )(apodization, echo, acquirer, counts, rows, columns)


def pick_acquirers(acquirer, pieces, copies):
    transmits = acquirer.shape[1]
    tile = pieces.shape[2:]

    def kernel(acquirer_ref, pieces_ref, out_ref):
        for transmit in range(transmits):
            chip = jnp.broadcast_to(acquirer_ref[:, transmit : transmit + 1], tile) // Z
            picked = [jnp.zeros(tile, jnp.float32)] * 2
            for source in range(pieces.shape[0]):
                picked = [
                    jnp.where(chip == source, pieces_ref[source, half], picked[half]) for half in range(2)
                ]
            for copy in range(copies):
                out_ref[copy, transmit] = picked[copy % 2]

    return pl.pallas_call(
        kernel,
        out_shape=jax.ShapeDtypeStruct((copies, transmits) + tile, pieces.dtype),
        in_specs=[VMEM] * 2,
        out_specs=VMEM,
        cost_estimate=pl.CostEstimate(flops=10_000_000_000, bytes_accessed=0, transcendentals=0),
        compiler_params=PARAMS,
    )(acquirer, pieces)


def sum_and_copy(acquirer, parts, groups, copies):
    transmits = acquirer.shape[1]
    tile = parts.shape[2:]

    def kernel(acquirer_ref, parts_ref, out_ref):
        for transmit in range(transmits):
            z = jnp.broadcast_to(acquirer_ref[:, transmit : transmit + 1], tile) & (Z - 1)
            total = jnp.zeros(tile, jnp.float32)
            for source in range(Z):
                here = parts_ref[source * groups, transmit]
                for group in range(1, groups):
                    here += parts_ref[source * groups + group, transmit]
                total = jnp.where(z == source, here, total)
            for copy in range(copies):
                out_ref[copy, transmit] = total

    return pl.pallas_call(
        kernel,
        out_shape=jax.ShapeDtypeStruct((copies,) + parts.shape[1:], parts.dtype),
        in_specs=[VMEM, VMEM],
        out_specs=VMEM,
        cost_estimate=pl.CostEstimate(flops=0, bytes_accessed=0, transcendentals=0),
        compiler_params=PARAMS,
    )(acquirer, parts)


def slot_sums(slot_table, windows_of_voxels, empty, table, panels, others):
    transmits, slots, block, _ = panels.shape[1:]
    quarters = 4
    row_blocks = windows_of_voxels.shape[0]
    windows = quarters * table.shape[2]
    pairs = table.shape[0] // quarters

    def kernel(
        slots_given, index_ref, empty_ref, table_ref, panels_ref, others_ref,
        out_ref, weights, total,
    ):
        group = lax.axis_index("grp")
        core = group & 1
        mine = (lax.broadcasted_iota(jnp.int32, (windows, LANES), 1) // (LANES // 2)) == core
        for transmit in range(transmits):
            for pair in range(pairs):
                both = jnp.concatenate(
                    [table_ref[pair * quarters + quarter, transmit] for quarter in range(quarters)], axis=0
                )
                for place, aligned in enumerate((both, pltpu.roll(both, LANES // 2, 1))):
                    aligned = jnp.where(mine, aligned, 0.0)
                    high = aligned.astype(jnp.bfloat16)
                    low = (aligned - high.astype(jnp.float32)).astype(jnp.bfloat16)
                    weights[(transmit * pairs + pair) * 2 + place] = jnp.concatenate([high, low], axis=0)
        total[...] = empty_ref[...]
        starts = (group * slots, (group ^ 1) * slots)
        nothing = jnp.zeros((2 * windows, LANES), jnp.bfloat16)
        for transmit in range(transmits):
            listed = slots_given[transmit]
            here = [pltpu.roll(listed, lax.rem(LANES - start, LANES), 1) for start in starts]
            for slot in range(slots):
                packed = [side[0, slot] for side in here]
                columns = [(number & ((1 << COLUMN_BITS) - 1)) ^ core for number in packed]
                own, other = (weights[transmit * pairs * 2 + column] for column in columns)
                terms = lax.dot_general(
                    jnp.concatenate(
                        [
                            jnp.concatenate([own, nothing], axis=1),
                            jnp.concatenate([nothing, other], axis=1),
                        ],
                        axis=0,
                    ),
                    jnp.concatenate(
                        [panels_ref[0, transmit, slot], others_ref[0, transmit, slot]], axis=1
                    ),
                    NT,
                    preferred_element_type=jnp.float32,
                )
                for i, number in enumerate(packed):
                    high, low = (
                        terms[(2 * i + j) * windows : (2 * i + j + 1) * windows] for j in range(2)
                    )
                    total[number >> COLUMN_BITS] += high + low
        number = lax.broadcasted_iota(jnp.int32, (windows, block), 0)
        for row in range(row_blocks):
            chosen = jnp.where(number == index_ref[row], total[row], 0.0)
            out_ref[row] = jnp.sum(chosen, axis=0, keepdims=True)

    return pl.pallas_call(
        kernel,
        out_shape=jax.ShapeDtypeStruct((row_blocks, 1, block), jnp.float32),
        in_specs=[VMEM] * 6,
        out_specs=VMEM,
        scratch_shapes=[
            pltpu.VMEM((transmits * pairs * 2, 2 * windows, LANES), jnp.bfloat16),
            pltpu.VMEM(empty.shape, empty.dtype),
        ],
        compiler_params=PARAMS,
    )(slot_table, windows_of_voxels, empty, table, panels, others)


def exchange(pieces, axis, lines=None):
    return lax.all_to_all(
        pieces, axis, split_axis=0, concat_axis=0, axis_index_groups=lines, tiled=True
    )


def per_device(
    echo_data, acquirer, panels, block_count, block_rows, block_columns, apodization, window_index
):
    slabs, groups = lax.axis_size("slab"), lax.axis_size("grp")
    planes = [list(range(z, slabs, Z)) for z in range(Z)]
    lines = [
        [(chip * Z + z) * groups + group for z in range(Z) for group in range(groups)]
        for chip in range(slabs // Z)
    ]
    voxels = window_index.reshape(-1, 1, panels.shape[-1])
    rows, columns = (jnp.transpose(v, (1, 0, 2)) for v in (block_rows, block_columns))
    empty = empty_sums(voxels.shape[0], apodization.shape[0], voxels.shape[2])
    acquirer = acquirer.reshape(1, -1)
    empty, apodization, echo_data, acquirer, block_count, rows, columns = lax.optimization_barrier(
        (empty, apodization, echo_data, acquirer, block_count, rows, columns)
    )
    sums, acquirer, slot_table = window_sums(
        apodization, echo_data, acquirer, block_count, rows, columns, voxels.shape[0]
    )
    sums, given = lax.optimization_barrier((sums, panels))
    others = lax.ppermute(given, "grp", [(i, i ^ 1) for i in range(groups)])
    pieces = exchange(sums, "slab", planes)
    picked = pick_acquirers(acquirer, pieces, Z * groups)
    parts = exchange(picked, ("slab", "grp"), lines)
    summed = sum_and_copy(acquirer, parts, groups, slabs // Z)
    summed, others = lax.optimization_barrier((summed, others))
    table = exchange(summed, "slab", planes)
    partial = slot_sums(slot_table, voxels, empty, table, panels, others)
    return jnp.sum(exchange(partial, "grp"), axis=(0, 1))


def solution(mesh):
    return jax.shard_map(
        per_device,
        mesh=mesh,
        in_specs=(
            P("slab", "grp", None),
            P(),
            P("slab", None, "grp", None, None),
            P("slab", None),
            P("slab", None, None),
            P("slab", None, None),
            P(None, "grp"),
            P("slab"),
        ),
        out_specs=P(("slab", "grp")),
        check_vma=False,
    )
```
